32 devices in a mesh: group: 2 (over y), seq: 4 (over z), fsdp: 4 (over x, core).
Axes of the slice: x: 2, y: 2, z: 4, core: 2. Of those that a mesh axis runs over, the one named last changes fastest.
Arguments:
- tile_patches: bfloat16 [64, 256, 1536], P(('group', 'seq', 'fsdp')), parts along dimension 0, may hold values from -6 to 6
- vit_gain: float32 [1536], replicated, may hold values from 0.25 to 1.75
- w_query: bfloat16 [1536, 768], P('fsdp'), may hold values from -0.15625 to 0.15625
- w_key: bfloat16 [1536, 768], P('fsdp'), may hold values from -0.15625 to 0.15625
- w_value: bfloat16 [1536, 768], P('fsdp'), may hold values from -0.15625 to 0.15625
- w_out: bfloat16 [768, 1536], P('fsdp'), may hold values from -0.21875 to 0.21875
- w_proj: bfloat16 [1536, 768], P('fsdp'), may hold values from -0.15625 to 0.15625
- long_gain: float32 [768], replicated, may hold values from 0.25 to 1.75
- long_query: bfloat16 [768, 768], P(None, 'fsdp'), may hold values from -0.21875 to 0.21875
- long_key: bfloat16 [768, 768], P(None, 'fsdp'), may hold values from -0.21875 to 0.21875
- long_value: bfloat16 [768, 768], P(None, 'fsdp'), may hold values from -0.21875 to 0.21875
- long_out: bfloat16 [768, 768], P('fsdp'), may hold values from -0.21875 to 0.21875
- seq_order: int32 [64], P(('group', 'seq', 'fsdp')), parts along dimension 0, may hold values from 0 to 31, each once
- counts: int32 [32], P(('group', 'seq', 'fsdp')), parts along dimension 0, may hold values from 1 to 2
Outputs:
- encoded: bfloat16 [64, 768], P(('group', 'seq'), 'fsdp'), parts along dimension 0
The draws below stay inside these ranges and needn't reach their ends.
There are 2 independent parts, one for each index of `group`. The reference program is written for one: setup_inputs(seed, part) draws one part's arguments, and reference() takes and returns one part's arrays. A program takes and returns all parts, laid end to end along the dimension named above; an argument that names none is the same for every part. Nothing has to cross between parts.
Inputs may be any that keep to these rules, and one draw needn't show every extreme that they name: `seq_order`: each of the 32 sequence positions belongs to exactly one tile. In each block of 2 consecutive tiles the first counts tiles are tissue.
All inputs are finite; a program needn't handle non-finite values.
Results may differ from the reference program's by a relative error of at most 0.013.
Values may be sent and summed in bfloat16 or wider, within the bound.
No kernel may reach another device: no remote copies, remote signals or barrier semaphores. Data moves between devices by JAX's collectives and lax.ppermute only.
A program may use at most 64 MiB of HBM per device.

```python
import math
import jax
import jax.numpy as jnp
from jax import lax

DV = 1536
VH = 12
VHD = 64
PATCH = 256
TILE_DEV = 2
D = 768
HEADS = 16
DILATION_STEP = 4
TILES = 32
N_SEQ = 4
N_FSDP = 4


def touch_ends(entries, own_key, smallest, top_value):
    dims = entries.shape
    spot = [jax.random.randint(jax.random.fold_in(own_key, axis), (), 0, dims[axis]) for axis in range(len(dims))]
    entries = entries.at[tuple(spot)].set(smallest)
    longest = dims.index(max(dims))
    spot[longest] = (spot[longest] + 1) % dims[longest]
    return entries.at[tuple(spot)].set(top_value)


def level_of(rng, shape, cuts, smallest, top_value):
    def one(axis_at, blocks):
        draws = jax.random.uniform(jax.random.fold_in(jax.random.fold_in(rng, 6), axis_at), (blocks,), jnp.float32, smallest / len(cuts), top_value / len(cuts))
        return jnp.repeat(jnp.exp(draws), shape[axis_at] // blocks).reshape((-1,) + (1,) * (len(shape) - axis_at - 1))

    loudness = one(*cuts[0])
    for cut in cuts[1:]:
        loudness = loudness * one(*cut)
    return loudness


def scatter_about(rng, shape, width, reach, shards=(), kind=jnp.bfloat16):
    gain = level_of(rng, shape, shards, -0.22, 0.18) if shards else 1.0
    array = jax.random.normal(rng, shape, jnp.float32) * width * gain
    return jnp.minimum(jnp.maximum(array, -reach), reach).astype(kind)


def setup_inputs(seed: int = 0, part: int = 0) -> dict:
    keys = jax.random.split(jax.random.key(seed), 15)
    part_keys = jax.random.split(jax.random.fold_in(keys[14], part), 15)
    tile_patches = scatter_about(part_keys[0], (TILES, PATCH, DV), 1.0, 6.0, ((0, 16),))
    vit_gain = jnp.clip(1.0 + 0.15 * jax.random.normal(keys[1], (DV,), jnp.float32), 0.25, 1.75)
    w_query = scatter_about(keys[2], (DV, VH * VHD), DV ** -0.5, 0.15625, ((0, 4),))
    w_key = scatter_about(keys[3], (DV, VH * VHD), DV ** -0.5, 0.15625, ((0, 4),))
    w_value = scatter_about(keys[4], (DV, VH * VHD), DV ** -0.5, 0.15625, ((0, 4),))
    w_out = scatter_about(keys[5], (VH * VHD, DV), (VH * VHD) ** -0.5, 0.21875, ((0, 4),))
    w_proj = scatter_about(keys[6], (DV, D), DV ** -0.5, 0.15625, ((0, 4),))
    long_gain = jnp.clip(1.0 + 0.15 * jax.random.normal(keys[7], (D,), jnp.float32), 0.25, 1.75)
    long_query = scatter_about(keys[8], (D, D), D ** -0.5, 0.21875, ((1, 4),))
    long_key = scatter_about(keys[9], (D, D), D ** -0.5, 0.21875, ((1, 4),))
    long_value = scatter_about(keys[10], (D, D), D ** -0.5, 0.21875, ((1, 4),))
    long_out = scatter_about(keys[11], (D, D), D ** -0.5, 0.21875, ((0, 4),))
    seq_order = jax.random.permutation(part_keys[12], TILES).astype(jnp.int32)
    counts = touch_ends(jax.random.randint(part_keys[13], (N_SEQ * N_FSDP,), 1, TILE_DEV + 1), jax.random.fold_in(part_keys[13], 1), 1, TILE_DEV).astype(jnp.int32)
    return {"tile_patches": tile_patches, "vit_gain": vit_gain, "w_query": w_query, "w_key": w_key, "w_value": w_value, "w_out": w_out, "w_proj": w_proj, "long_gain": long_gain, "long_query": long_query, "long_key": long_key, "long_value": long_value, "long_out": long_out, "seq_order": seq_order, "counts": counts}


EPSILON = 1e-06

def layer_norm(inputs, norm_gain):
    widened = inputs.astype(jnp.float32)
    average = lax.optimization_barrier(jnp.mean(widened, axis=-1, keepdims=True))
    centred = widened - average
    variance = lax.optimization_barrier(jnp.mean(centred * centred, axis=-1, keepdims=True))
    return (centred * lax.rsqrt(variance + EPSILON) * norm_gain).astype(jnp.bfloat16)

def dilated_attention(query_rows, key_rows, value_rows, query_position_index, key_position_index, key_present, leading_head, head_total_count, segment):
    head_size = query_rows.shape[1] // head_total_count
    query_heads = query_rows.reshape(query_rows.shape[0], head_total_count, head_size).astype(jnp.float32)
    key_heads = key_rows.reshape(key_rows.shape[0], head_total_count, head_size).astype(jnp.float32)
    value_heads = value_rows.reshape(value_rows.shape[0], head_total_count, head_size).astype(jnp.float32)
    scores = jnp.einsum('rhd,khd->hrk', query_heads, key_heads) / math.sqrt(head_size)
    itself = query_position_index[:, None] == key_position_index[None, :]
    permitted_mask = (key_present[None, :] > 0) | itself
    in_local = (query_position_index[:, None] // segment == key_position_index[None, :] // segment) & permitted_mask
    head_shift_amounts = (leading_head + jnp.arange(head_total_count, dtype=jnp.int32)) % DILATION_STEP
    within_dilated_set = ((query_position_index % DILATION_STEP)[None, :, None] == head_shift_amounts[:, None, None]) & ((key_position_index % DILATION_STEP)[None, None, :] == head_shift_amounts[:, None, None]) & permitted_mask[None]
    lifted = jnp.exp(scores)
    local_weights = jnp.where(in_local[None], lifted, 0.0)
    dilated_weights = jnp.where(within_dilated_set, lifted, 0.0)
    denominator = lax.optimization_barrier(jnp.sum(local_weights, axis=-1)) + lax.optimization_barrier(jnp.sum(dilated_weights, axis=-1))
    numerator = jnp.einsum('hrk,khd->rhd', local_weights.astype(jnp.bfloat16).astype(jnp.float32), value_heads)
    numerator = numerator + jnp.einsum('hrk,khd->rhd', dilated_weights.astype(jnp.bfloat16).astype(jnp.float32), value_heads)
    combined = numerator / jnp.transpose(denominator)[:, :, None]
    return combined.reshape(query_rows.shape[0], head_total_count * head_size).astype(jnp.bfloat16)

def reference(tile_patches, vit_gain, w_query, w_key, w_value, w_out, w_proj, long_gain, long_query, long_key, long_value, long_out, seq_order, counts):

    def encode(one_tile):
        normed = layer_norm(one_tile, vit_gain)
        key_rows = jnp.dot(normed, w_key, preferred_element_type=jnp.float32)
        value_rows = jnp.dot(normed, w_value, preferred_element_type=jnp.float32)
        query_row = jnp.dot(normed[0:1], w_query, preferred_element_type=jnp.float32).astype(jnp.bfloat16)
        query_heads = query_row.reshape(VH, VHD).astype(jnp.float32)
        key_heads = key_rows.reshape(PATCH, VH, VHD)
        scores = jnp.einsum('hd,phd->hp', query_heads, key_heads, precision=lax.Precision.HIGHEST) / math.sqrt(VHD)
        lifted = jnp.exp(scores)
        attn_probs = (lifted / lax.optimization_barrier(jnp.sum(lifted, axis=-1, keepdims=True))).astype(jnp.bfloat16)
        value_heads = value_rows.reshape(PATCH, VH, VHD)
        pooled = jnp.einsum('hp,phd->hd', attn_probs.astype(jnp.float32), value_heads, precision=lax.Precision.HIGHEST).reshape(1, VH * VHD).astype(jnp.bfloat16)
        class_row = (one_tile[0:1].astype(jnp.float32) + jnp.dot(pooled, w_out, preferred_element_type=jnp.float32)).astype(jnp.bfloat16)
        return jnp.dot(class_row, w_proj, preferred_element_type=jnp.float32)[0].astype(jnp.bfloat16)
    embeds = lax.map(encode, tile_patches)
    tile_index = jnp.arange(TILES, dtype=jnp.int32)
    present = (tile_index % TILE_DEV < counts[tile_index // TILE_DEV]).astype(jnp.int32)
    embeds = jnp.where(present[:, None] > 0, embeds, jnp.zeros_like(embeds))
    sequence = jnp.zeros((TILES, D), jnp.bfloat16).at[seq_order].set(embeds)
    seq_present = jnp.zeros((TILES,), jnp.int32).at[seq_order].set(present)
    long_normed = layer_norm(sequence, long_gain)
    query_rows = jnp.dot(long_normed, long_query, preferred_element_type=jnp.float32).astype(jnp.bfloat16)
    key_rows = jnp.dot(long_normed, long_key, preferred_element_type=jnp.float32).astype(jnp.bfloat16)
    value_rows = jnp.dot(long_normed, long_value, preferred_element_type=jnp.float32).astype(jnp.bfloat16)
    positions = jnp.arange(TILES, dtype=jnp.int32)
    attended = dilated_attention(query_rows, key_rows, value_rows, positions, positions, seq_present, 0, HEADS, TILES // 4)
    return (sequence.astype(jnp.float32) + jnp.dot(attended, long_out, preferred_element_type=jnp.float32)).astype(jnp.bfloat16)
```

```python
import functools
import math

import jax
import jax.numpy as jnp
from jax import lax
from jax.experimental import pallas as pl
from jax.experimental.pallas import tpu as pltpu
from jax.sharding import PartitionSpec as P

VHD = 64
HEADS = 16
DILATION_STEP = 4
EPSILON = 1e-06
LANES = 128


BF16 = jnp.bfloat16
F32 = jnp.float32


def other(index, step, size):
    return index ^ step if size & (size - 1) == 0 else (index + step) % size


def source(index, step, size):
    return index ^ step if size & (size - 1) == 0 else (index + size - step) % size


def swap(array, axis, step):
    size = lax.axis_size(axis)
    return lax.ppermute(array, axis, [(i, other(i, step, size)) for i in range(size)])


def spread(array, axis):
    return [array] + [swap(array, axis, step) for step in range(1, lax.axis_size(axis))]


def deal(arrays, axis):
    return [arrays[0]] + [swap(arrays[step], axis, step) for step in range(1, len(arrays))]


def normalise(rows, gain):
    average = jnp.mean(rows, axis=-1, keepdims=True)
    centred = rows - average
    variance = jnp.mean(centred * centred, axis=-1, keepdims=True)
    return (centred * lax.rsqrt(variance + EPSILON) * gain).astype(BF16)


def contract(left, right, left_axis, right_axis):
    return lax.dot_general(
        left, right, (((left_axis,), (right_axis,)), ((), ())), preferred_element_type=F32
    )


def call(body, outs, scratch=(), name=None):
    def run(place, *arrays):
        return pl.pallas_call(
            body,
            out_shape=outs,
            in_specs=[pl.BlockSpec(memory_space=pltpu.SMEM)]
            + [pl.BlockSpec(memory_space=pltpu.VMEM)] * len(arrays),
            out_specs=jax.tree.map(lambda _: pl.BlockSpec(memory_space=pltpu.VMEM), outs),
            scratch_shapes=list(scratch),
            name=name,
        )(place, *arrays)

    return run


def query_kernel(size, place, *refs):
    heads_in, (gain, weight, out, first, notes, rows, blocks) = refs[:size], refs[size:]
    me = place[0]
    tiles = heads_in[0].shape[0]
    width = gain.shape[1]
    mine = weight.shape[0]
    for step in range(size):
        rows[source(me, step, size)] = heads_in[step][...].astype(F32)
    full = rows[...].reshape(size * tiles, rows.shape[2])
    notes[...] = full[:, width:]
    full = full[:, :width]
    for block in range(size):
        blocks[block] = full[:, block * mine : (block + 1) * mine]
    first[...] = blocks[me]
    normed = normalise(full, gain[...]).astype(F32)
    for block in range(size):
        blocks[block] = normed[:, block * mine : (block + 1) * mine]
    out[...] = contract(blocks[me].astype(BF16), weight[...], 1, 0).astype(BF16)


def fold_kernel(size, padded, place, *refs):
    parts, weight, outs, folded = refs[:size], refs[size], refs[size + 1 : -1], refs[-1]
    me = place[0]
    total = parts[0][...].astype(F32)
    for step in range(1, size):
        total = total + parts[step][...].astype(F32)
    query = total.astype(BF16).astype(F32)
    count, width = query.shape
    spread_query = jnp.broadcast_to(query[:, None, :], (count, padded, width))
    head = lax.broadcasted_iota(jnp.int32, (count, padded, width), 1)
    column = lax.broadcasted_iota(jnp.int32, (count, padded, width), 2)
    blocked = jnp.where(column // VHD == head, spread_query, 0.0)
    blocked = blocked.reshape(count * padded, width).astype(BF16)
    folded[...] = contract(blocked, weight[...], 1, 1).astype(BF16).reshape(folded.shape)
    for step in range(size):
        outs[step][...] = folded[other(me, step, size)]


def token_kernel(size, padded, place, *refs):
    parts, normed, outs, (blocks, folded) = (
        refs[:size],
        refs[size],
        refs[size + 1 : -2],
        refs[-2:],
    )
    me = place[0]
    rows = parts[0].shape[1]
    for step in range(size):
        blocks[source(me, step, size)] = parts[step][...]
    for block in range(size):
        folded[:, block * rows : (block + 1) * rows] = blocks[block]
    for tile in range(normed.shape[0]):
        tokens = normed[tile]
        at = slice(tile * padded, (tile + 1) * padded)
        scores = contract(folded[at, :], tokens, 1, 1) / math.sqrt(VHD)
        lifted = jnp.exp(scores)
        probs = (lifted / jnp.sum(lifted, axis=-1, keepdims=True)).astype(BF16)
        mixed = contract(probs, tokens, 1, 0).astype(BF16)
        for block in range(size):
            blocks[block, at] = mixed[:, block * rows : (block + 1) * rows]
    for step in range(size):
        outs[step][...] = blocks[other(me, step, size)]


def value_kernel(size, padded, place, *refs):
    parts, (weight, out, mixed) = refs[:size], refs[size:]
    me = place[0]
    for step in range(size):
        mixed[source(me, step, size)] = parts[step][...]
    rows = mixed[...].reshape(size * parts[0].shape[0], parts[0].shape[1])
    product = contract(rows, weight[...], 1, 0)
    count, width = product.shape[0] // padded, product.shape[1]
    product = product.reshape(count, padded, width)
    head = lax.broadcasted_iota(jnp.int32, (count, padded, width), 1)
    column = lax.broadcasted_iota(jnp.int32, (count, padded, width), 2)
    kept = jnp.where(column // VHD == head, product, 0.0)
    out[...] = jnp.sum(kept, axis=1).astype(BF16)


def embed_kernel(size, place, *refs):
    parts, blocks, (first, project, out, weight) = (
        refs[:size],
        refs[size : 2 * size],
        refs[2 * size :],
    )
    me = place[0]
    total = parts[0][...].astype(F32)
    for step in range(1, size):
        total = total + parts[step][...].astype(F32)
    pooled = total.astype(BF16)
    depth = blocks[0].shape[0]
    for step in range(size):
        start = pl.multiple_of(source(me, step, size) * depth, 16)
        weight[pl.ds(start, depth), :] = blocks[step][...]
    class_row = (first[...] + contract(pooled, weight[...], 1, 0)).astype(BF16)
    out[...] = contract(class_row, project[...], 1, 0).astype(BF16)


def gather_kernel(size, place, *refs):
    parts, (notes, out) = refs[:size], refs[size:]
    total = parts[0][...].astype(F32)
    for step in range(1, size):
        total = total + parts[step][...].astype(F32)
    width = total.shape[1]
    out[:, :width] = jnp.where(notes[:, 2:3] > 0, total, 0.0).astype(BF16)
    out[:, width:] = notes[...].astype(BF16)


def slide_kernel(size, seq_size, place, *refs):
    parts = refs[:seq_size]
    gain, w_query, w_key, w_value, w_out = refs[seq_size : seq_size + 5]
    outs, (long_normed,) = refs[seq_size + 5 : -1], refs[-1:]
    me, seq = place[0], place[1]
    rows = parts[0].shape[0]
    model = gain.shape[1]
    width = w_query.shape[1]
    total = rows * seq_size
    segment = total // 4
    tiles = jnp.concatenate([part[...].astype(F32) for part in parts], axis=0)
    notes = tiles[:, model:]
    order = notes[:, 0:1] * 256.0 + notes[:, 1:2]
    spots = lax.broadcasted_iota(jnp.int32, (total, total), 1).astype(F32)
    picker = jnp.where(order == spots, 1.0, 0.0)
    picked = contract(picker.astype(BF16), tiles.astype(BF16), 0, 0)
    long_normed[...] = normalise(picked[:, :model], gain[...]).astype(F32)
    normed = long_normed[...].astype(BF16)
    mine = pl.ds(pl.multiple_of(seq * rows, 8), rows)
    queries = contract(long_normed[mine, :].astype(BF16), w_query[...], 1, 0).astype(BF16)
    keys = contract(normed, w_key[...], 1, 0).astype(BF16)
    values = contract(normed, w_value[...], 1, 0).astype(BF16)
    here = jnp.sum(jnp.where(order == spots, notes[:, 2:3], 0.0), axis=0, keepdims=True)
    head_size = model // HEADS
    count = width // head_size
    shape = (count, rows, width)
    owner = lax.broadcasted_iota(jnp.int32, shape, 2) // head_size
    own = owner == lax.broadcasted_iota(jnp.int32, shape, 0)
    blocked = jnp.where(own, jnp.broadcast_to(queries.astype(F32)[None], shape), 0.0)
    blocked = blocked.reshape(count * rows, width).astype(BF16)
    scores = contract(blocked, keys, 1, 1) / math.sqrt(head_size)
    line = lax.broadcasted_iota(jnp.int32, (count * rows, total), 0)
    asking = seq * rows + line % rows
    shift = (me * count + line // rows) % DILATION_STEP
    key_at = lax.broadcasted_iota(jnp.int32, (count * rows, total), 1)
    allowed = (here > 0) | (asking == key_at)
    near = (asking // segment == key_at // segment) & allowed
    far = (asking % DILATION_STEP == shift) & (key_at % DILATION_STEP == shift) & allowed
    times = jnp.where(near, 1.0, 0.0) + jnp.where(far, 1.0, 0.0)
    lifted = jnp.where(times > 0, jnp.exp(scores), 0.0)
    bottom = jnp.sum(lifted * times, axis=-1, keepdims=True)
    weights = (lifted.astype(BF16).astype(F32) * times).astype(BF16)
    mixed = (contract(weights, values, 1, 0) / bottom).reshape(shape)
    attended = jnp.sum(jnp.where(own, mixed, 0.0), axis=0).astype(BF16)
    for step in range(size):
        outs[step][...] = contract(attended, w_out[other(me, step, size)], 1, 0).astype(BF16)
    tail = outs[size]
    residual = jnp.zeros((rows, width), F32)
    long_normed[...] = picked[:, :model]
    at_home = long_normed[mine, :]
    for block in range(size):
        residual = jnp.where(me == block, at_home[:, block * width : (block + 1) * width], residual)
    tail[...] = residual


def local(
    tile_patches,
    vit_gain,
    w_query,
    w_key,
    w_value,
    w_out,
    w_proj,
    long_gain,
    long_query,
    long_key,
    long_value,
    long_out,
    seq_order,
    counts,
):
    size = lax.axis_size("fsdp")
    seq_size = lax.axis_size("seq")
    me = lax.axis_index("fsdp")
    place = jnp.stack([me, lax.axis_index("seq")]).astype(jnp.int32)
    tiles, patches, width = tile_patches.shape
    vit_width = w_key.shape[1]
    heads = vit_width // VHD
    padded = -(-heads // 16) * 16
    rows = w_key.shape[0]
    model = w_proj.shape[1]
    depth = w_out.shape[0]
    count = tiles * size

    slot = jnp.arange(tiles, dtype=jnp.int32)
    present = (slot < counts[0]).astype(jnp.int32)
    lane = jnp.arange(LANES, dtype=jnp.int32)[None, :]
    notes = jnp.where(
        lane == 0,
        (seq_order // 256)[:, None],
        jnp.where(
            lane == 1,
            (seq_order % 256)[:, None],
            jnp.where(lane == 2, present[:, None], 0),
        ),
    ).astype(BF16)
    head_rows = spread(jnp.concatenate([tile_patches[:, 0, :], notes], axis=1), "fsdp")

    normed = normalise(tile_patches.astype(F32), vit_gain)

    gain_row = vit_gain[None, :]
    query_part, first, notes = call(
        functools.partial(query_kernel, size),
        [
            jax.ShapeDtypeStruct((count, vit_width), BF16),
            jax.ShapeDtypeStruct((count, rows), F32),
            jax.ShapeDtypeStruct((count, LANES), F32),
        ],
        [pltpu.VMEM((size, tiles, width + LANES), F32), pltpu.VMEM((size, count, rows), F32)],
        name="query",
    )(place, *head_rows, gain_row, w_query)
    query_parts = spread(query_part, "fsdp")

    block = jax.ShapeDtypeStruct((tiles * padded, rows), BF16)
    folded = call(
        functools.partial(fold_kernel, size, padded),
        [block] * size,
        [pltpu.VMEM((size, tiles * padded, rows), BF16)],
        name="fold",
    )(place, *query_parts, w_key)
    folded = deal(folded, "fsdp")

    out_blocks = jnp.transpose(w_out.reshape(depth, size, width // size), (1, 0, 2))
    out_blocks = deal(
        [
            lax.dynamic_index_in_dim(out_blocks, other(me, step, size), 0, keepdims=False)
            for step in range(size)
        ],
        "fsdp",
    )

    mixed = call(
        functools.partial(token_kernel, size, padded),
        [block] * size,
        [pltpu.VMEM((size, tiles * padded, rows), BF16), pltpu.VMEM((tiles * padded, width), BF16)],
        name="tokens",
    )(place, *folded, normed)
    mixed = deal(mixed, "fsdp")

    pooled_part = call(
        functools.partial(value_kernel, size, padded),
        jax.ShapeDtypeStruct((count, vit_width), BF16),
        [pltpu.VMEM((size, tiles * padded, rows), BF16)],
        name="value",
    )(place, *mixed, w_value)
    pooled_parts = spread(pooled_part, "fsdp")

    embed_part = call(
        functools.partial(embed_kernel, size),
        jax.ShapeDtypeStruct((count, model), BF16),
        [pltpu.VMEM((vit_width, width // size), BF16)],
        name="embed",
    )(place, *pooled_parts, *out_blocks, first, w_proj)
    embed_parts = spread(embed_part, "fsdp")

    group_tiles = call(
        functools.partial(gather_kernel, size),
        jax.ShapeDtypeStruct((count, model + LANES), BF16),
        name="gather",
    )(place, *embed_parts, notes)
    all_tiles = spread(group_tiles, "seq")

    head_width = long_query.shape[1]
    long_blocks = jnp.transpose(long_out.reshape(head_width, size, head_width), (1, 0, 2))
    outs = [jax.ShapeDtypeStruct((count, head_width), BF16)] * size + [
        jax.ShapeDtypeStruct((count, head_width), F32)
    ]
    *terms, residual = call(
        functools.partial(slide_kernel, size, seq_size),
        outs,
        [pltpu.VMEM((count * seq_size, model), F32)],
        name="slide",
    )(place, *all_tiles, long_gain[None, :], long_query, long_key, long_value, long_blocks)
    terms = deal(terms, "fsdp")
    summed = terms[0].astype(F32)
    for step in range(1, size):
        summed = summed + terms[step].astype(F32)
    return (residual + summed).astype(BF16)


def solution(mesh):
    return jax.shard_map(
        local,
        mesh=mesh,
        in_specs=(
            P(("group", "seq", "fsdp"), None, None),
            P(),
            P("fsdp", None),
            P("fsdp", None),
            P("fsdp", None),
            P("fsdp", None),
            P("fsdp", None),
            P(),
            P(None, "fsdp"),
            P(None, "fsdp"),
            P(None, "fsdp"),
            P("fsdp", None),
            P(("group", "seq", "fsdp")),
            P(("group", "seq", "fsdp")),
        ),
        out_specs=P(("group", "seq"), "fsdp"),
        check_vma=False,
    )
```

```python
import functools
import math

import jax
import jax.numpy as jnp
from jax import lax
from jax.experimental import pallas as pl
from jax.experimental.pallas import tpu as pltpu
from jax.sharding import PartitionSpec as P

VHD = 64
HEADS = 16
DILATION_STEP = 4
EPSILON = 1e-06
LANES = 128


BF16 = jnp.bfloat16
F32 = jnp.float32


def other(index, step, size):
    return index ^ step if size & (size - 1) == 0 else (index + step) % size


def source(index, step, size):
    return index ^ step if size & (size - 1) == 0 else (index + size - step) % size


def swap(array, axis, step):
    size = lax.axis_size(axis)
    return lax.ppermute(array, axis, [(i, other(i, step, size)) for i in range(size)])


def spread(array, axis):
    return [array] + [swap(array, axis, step) for step in range(1, lax.axis_size(axis))]


def deal(arrays, axis):
    return [arrays[0]] + [swap(arrays[step], axis, step) for step in range(1, len(arrays))]


def normalise(rows, gain):
    average = jnp.mean(rows, axis=-1, keepdims=True)
    centred = rows - average
    variance = jnp.mean(centred * centred, axis=-1, keepdims=True)
    return (centred * lax.rsqrt(variance + EPSILON) * gain).astype(BF16)


def contract(left, right, left_axis, right_axis):
    return lax.dot_general(
        left, right, (((left_axis,), (right_axis,)), ((), ())), preferred_element_type=F32
    )


def in_hbm(array):
    return pltpu.with_memory_space_constraint(array, pltpu.HBM)


def call(body, outs, scratch=(), name=None, limit=1 << 23):
    def run(place, *arrays):
        return pl.pallas_call(
            body,
            out_shape=outs,
            in_specs=[pl.BlockSpec(memory_space=pltpu.SMEM)]
            + [pl.BlockSpec(memory_space=pltpu.VMEM)] * len(arrays),
            out_specs=jax.tree.map(lambda _: pl.BlockSpec(memory_space=pltpu.VMEM), outs),
            scratch_shapes=list(scratch),
            compiler_params=pltpu.CompilerParams(vmem_limit_bytes=limit),
            name=name,
        )(place, *arrays)

    return run


def head_kernel(order, counts, tokens, out):
    width = tokens.shape[2]
    lane = lax.broadcasted_iota(jnp.int32, (1, LANES), 1)
    for tile in range(tokens.shape[0]):
        spot = order[tile]
        present = (counts[0] > tile).astype(jnp.int32)
        high = jnp.where(lane == 0, spot // 256, 0)
        low = jnp.where(lane == 1, spot % 256, 0)
        notes = high + low + jnp.where(lane == 2, present, 0)
        out[tile : tile + 1, :width] = tokens[tile, 0:1, :]
        out[tile : tile + 1, width:] = notes.astype(F32).astype(BF16)


def query_kernel(size, place, *refs):
    heads_in, (gain, weight, out, first, notes, rows, blocks) = refs[:size], refs[size:]
    me = place[0] % size
    tiles = heads_in[0].shape[0]
    width = gain.shape[1]
    mine = weight.shape[0]
    for step in range(size):
        rows[source(me, step, size)] = heads_in[step][...].astype(F32)
    full = rows[...].reshape(size * tiles, rows.shape[2])
    notes[...] = full[:, width:]
    full = full[:, :width]
    for block in range(size):
        blocks[block] = full[:, block * mine : (block + 1) * mine]
    first[...] = blocks[me]
    normed = normalise(full, gain[...]).astype(F32)
    for block in range(size):
        blocks[block] = normed[:, block * mine : (block + 1) * mine]
    out[...] = contract(blocks[me].astype(BF16), weight[...], 1, 0).astype(BF16)


def fold_kernel(size, padded, place, *refs):
    parts, weight, outs, folded = refs[:size], refs[size], refs[size + 1 : -1], refs[-1]
    me = place[0] % size
    total = parts[0][...].astype(F32)
    for step in range(1, size):
        total = total + parts[step][...].astype(F32)
    query = total.astype(BF16).astype(F32)
    count, width = query.shape
    spread_query = jnp.broadcast_to(query[:, None, :], (count, padded, width))
    head = lax.broadcasted_iota(jnp.int32, (count, padded, width), 1)
    column = lax.broadcasted_iota(jnp.int32, (count, padded, width), 2)
    blocked = jnp.where(column // VHD == head, spread_query, 0.0)
    blocked = blocked.reshape(count * padded, width).astype(BF16)
    folded[...] = contract(blocked, weight[...], 1, 1).astype(BF16).reshape(folded.shape)
    for step in range(size):
        outs[step][...] = folded[other(me, step, size)]


def cut_kernel(size, place, weight, after, *refs):
    outs, blocks = refs[:-1], refs[-1]
    me = place[0] % size
    mine = weight.shape[1] // size
    for block in range(size):
        blocks[block] = weight[:, block * mine : (block + 1) * mine]
    for step in range(size):
        outs[step][...] = blocks[other(me, step, size)]


def token_kernel(size, padded, place, *refs):
    parts, normed, outs, (blocks, folded) = (
        refs[:size],
        refs[size],
        refs[size + 1 : -2],
        refs[-2:],
    )
    me = place[0] % size
    rows = parts[0].shape[1]
    for step in range(size):
        blocks[source(me, step, size)] = parts[step][...]
    for block in range(size):
        folded[:, block * rows : (block + 1) * rows] = blocks[block]
    for tile in range(normed.shape[0]):
        tokens = normed[tile]
        at = slice(tile * padded, (tile + 1) * padded)
        scores = contract(folded[at, :], tokens, 1, 1) / math.sqrt(VHD)
        lifted = jnp.exp(scores)
        probs = (lifted / jnp.sum(lifted, axis=-1, keepdims=True)).astype(BF16)
        mixed = contract(probs, tokens, 1, 0).astype(BF16)
        for block in range(size):
            blocks[block, at] = mixed[:, block * rows : (block + 1) * rows]
    for step in range(size):
        outs[step][...] = blocks[other(me, step, size)]


def value_kernel(size, padded, place, *refs):
    parts, (weight, out, mixed) = refs[:size], refs[size:]
    me = place[0] % size
    for step in range(size):
        mixed[source(me, step, size)] = parts[step][...]
    rows = mixed[...].reshape(size * parts[0].shape[0], parts[0].shape[1])
    product = contract(rows, weight[...], 1, 0)
    count, width = product.shape[0] // padded, product.shape[1]
    product = product.reshape(count, padded, width)
    head = lax.broadcasted_iota(jnp.int32, (count, padded, width), 1)
    column = lax.broadcasted_iota(jnp.int32, (count, padded, width), 2)
    kept = jnp.where(column // VHD == head, product, 0.0)
    out[...] = jnp.sum(kept, axis=1).astype(BF16)


def embed_kernel(size, place, *refs):
    parts, blocks, (first, project, out, weight) = (
        refs[:size],
        refs[size : 2 * size],
        refs[2 * size :],
    )
    me = place[0] % size
    total = parts[0][...].astype(F32)
    for step in range(1, size):
        total = total + parts[step][...].astype(F32)
    pooled = total.astype(BF16)
    depth = blocks[0].shape[0]
    for step in range(size):
        start = pl.multiple_of(source(me, step, size) * depth, 16)
        weight[pl.ds(start, depth), :] = blocks[step][...]
    class_row = (first[...] + contract(pooled, weight[...], 1, 0)).astype(BF16)
    out[...] = contract(class_row, project[...], 1, 0).astype(BF16)


def gather_kernel(size, place, *refs):
    parts, (notes, out) = refs[:size], refs[size:]
    total = parts[0][...].astype(F32)
    for step in range(1, size):
        total = total + parts[step][...].astype(F32)
    width = total.shape[1]
    out[:, :width] = jnp.where(notes[:, 2:3] > 0, total, 0.0).astype(BF16)
    out[:, width:] = notes[...].astype(BF16)


def slide_kernel(size, seq_size, place, *refs):
    parts = refs[:seq_size]
    gain, w_query, w_key, w_value, w_out = refs[seq_size : seq_size + 5]
    outs, (long_normed, blocks) = refs[seq_size + 5 : -2], refs[-2:]
    me, seq = place[0] % size, place[0] // size
    rows = parts[0].shape[0]
    model = gain.shape[1]
    width = w_query.shape[0]
    total = rows * seq_size
    segment = total // 4
    tiles = jnp.concatenate([part[...].astype(F32) for part in parts], axis=0)
    notes = tiles[:, model:]
    order = notes[:, 0:1] * 256.0 + notes[:, 1:2]
    spots = lax.broadcasted_iota(jnp.int32, (total, total), 1).astype(F32)
    picker = jnp.where(order == spots, 1.0, 0.0)
    picked = contract(picker.astype(BF16), tiles.astype(BF16), 0, 0)
    long_normed[...] = normalise(picked[:, :model], gain[...]).astype(F32)
    normed = long_normed[...].astype(BF16)
    mine = pl.ds(pl.multiple_of(seq * rows, 8), rows)
    queries = contract(long_normed[mine, :].astype(BF16), w_query[...], 1, 1).astype(BF16)
    keys = contract(normed, w_key[...], 1, 1).astype(BF16)
    values = contract(normed, w_value[...], 1, 1).astype(BF16)
    here = jnp.sum(jnp.where(order == spots, notes[:, 2:3], 0.0), axis=0, keepdims=True)
    head_size = model // HEADS
    count = width // head_size
    shape = (count, rows, width)
    owner = lax.broadcasted_iota(jnp.int32, shape, 2) // head_size
    own = owner == lax.broadcasted_iota(jnp.int32, shape, 0)
    blocked = jnp.where(own, jnp.broadcast_to(queries.astype(F32)[None], shape), 0.0)
    blocked = blocked.reshape(count * rows, width).astype(BF16)
    scores = contract(blocked, keys, 1, 1) / math.sqrt(head_size)
    line = lax.broadcasted_iota(jnp.int32, (count * rows, total), 0)
    asking = seq * rows + line % rows
    shift = (me * count + line // rows) % DILATION_STEP
    key_at = lax.broadcasted_iota(jnp.int32, (count * rows, total), 1)
    allowed = (here > 0) | (asking == key_at)
    near = (asking // segment == key_at // segment) & allowed
    far = (asking % DILATION_STEP == shift) & (key_at % DILATION_STEP == shift) & allowed
    times = jnp.where(near, 1.0, 0.0) + jnp.where(far, 1.0, 0.0)
    lifted = jnp.where(times > 0, jnp.exp(scores), 0.0)
    bottom = jnp.sum(lifted * times, axis=-1, keepdims=True)
    weights = (lifted.astype(BF16).astype(F32) * times).astype(BF16)
    mixed = (contract(weights, values, 1, 0) / bottom).reshape(shape)
    attended = jnp.sum(jnp.where(own, mixed, 0.0), axis=0).astype(BF16)
    terms = contract(attended, w_out[...], 1, 0)
    for block in range(size):
        blocks[block] = terms[:, block * width : (block + 1) * width]
    for step in range(size):
        outs[step][...] = blocks[other(me, step, size)].astype(BF16)
    long_normed[...] = picked[:, :model]
    at_home = long_normed[mine, :]
    for block in range(size):
        blocks[block] = at_home[:, block * width : (block + 1) * width]
    outs[size][...] = blocks[me]


def local(
    tile_patches,
    vit_gain,
    w_query,
    w_key,
    w_value,
    w_out,
    w_proj,
    long_gain,
    long_query,
    long_key,
    long_value,
    long_out,
    seq_order,
    counts,
):
    size = lax.axis_size("fsdp")
    seq_size = lax.axis_size("seq")
    me = lax.axis_index("fsdp")
    place = (lax.axis_index("seq") * size + me).astype(jnp.int32).reshape(1)
    tiles, patches, width = tile_patches.shape
    vit_width = w_key.shape[1]
    heads = vit_width // VHD
    padded = -(-heads // 16) * 16
    rows = w_key.shape[0]
    model = w_proj.shape[1]
    depth = w_out.shape[0]
    count = tiles * size

    head_row = pl.pallas_call(
        head_kernel,
        out_shape=jax.ShapeDtypeStruct((tiles, width + LANES), BF16),
        grid=(1,),
        in_specs=[
            pl.BlockSpec(memory_space=pltpu.SMEM),
            pl.BlockSpec(memory_space=pltpu.SMEM),
            pl.BlockSpec((tiles, 8, width), lambda i: (0, 0, 0)),
        ],
        out_specs=pl.BlockSpec(memory_space=pltpu.VMEM),
        compiler_params=pltpu.CompilerParams(vmem_limit_bytes=1 << 20),
        name="head",
    )(in_hbm(seq_order), counts, in_hbm(tile_patches))
    head_rows = spread(head_row, "fsdp")

    normed = normalise(tile_patches.astype(F32), vit_gain)

    gain_row = vit_gain[None, :]
    query_part, first, notes = call(
        functools.partial(query_kernel, size),
        [
            jax.ShapeDtypeStruct((count, vit_width), BF16),
            jax.ShapeDtypeStruct((count, rows), F32),
            jax.ShapeDtypeStruct((count, LANES), F32),
        ],
        [pltpu.VMEM((size, tiles, width + LANES), F32), pltpu.VMEM((size, count, rows), F32)],
        name="query",
    )(place, *head_rows, gain_row, w_query)
    query_parts = spread(query_part, "fsdp")

    block = jax.ShapeDtypeStruct((tiles * padded, rows), BF16)
    folded = call(
        functools.partial(fold_kernel, size, padded),
        [block] * size,
        [pltpu.VMEM((size, tiles * padded, rows), BF16)],
        name="fold",
    )(place, *query_parts, w_key)
    out_blocks = call(
        functools.partial(cut_kernel, size),
        [jax.ShapeDtypeStruct((depth, width // size), BF16)] * size,
        [pltpu.VMEM((size, depth, width // size), BF16)],
        name="cut",
    )(place, w_out, folded[0])
    out_blocks = deal(out_blocks, "fsdp")
    folded = deal(folded, "fsdp")

    mixed = call(
        functools.partial(token_kernel, size, padded),
        [block] * size,
        [pltpu.VMEM((size, tiles * padded, rows), BF16), pltpu.VMEM((tiles * padded, width), BF16)],
        name="tokens",
    )(place, *folded, normed)
    mixed = deal(mixed, "fsdp")

    pooled_part = call(
        functools.partial(value_kernel, size, padded),
        jax.ShapeDtypeStruct((count, vit_width), BF16),
        [pltpu.VMEM((size, tiles * padded, rows), BF16)],
        name="value",
    )(place, *mixed, w_value)
    pooled_parts = spread(pooled_part, "fsdp")

    embed_part = call(
        functools.partial(embed_kernel, size),
        jax.ShapeDtypeStruct((count, model), BF16),
        [pltpu.VMEM((vit_width, width // size), BF16)],
        name="embed",
    )(place, *pooled_parts, *out_blocks, first, w_proj)
    embed_parts = spread(embed_part, "fsdp")

    group_tiles = call(
        functools.partial(gather_kernel, size),
        jax.ShapeDtypeStruct((count, model + LANES), BF16),
        name="gather",
    )(place, *embed_parts, notes)
    all_tiles = spread(group_tiles, "seq")

    head_width = long_query.shape[1]
    outs = [jax.ShapeDtypeStruct((count, head_width), BF16)] * size + [
        jax.ShapeDtypeStruct((count, head_width), F32)
    ]
    *terms, residual = call(
        functools.partial(slide_kernel, size, seq_size),
        outs,
        [
            pltpu.VMEM((count * seq_size, model), F32),
            pltpu.VMEM((size, count, head_width), F32),
        ],
        name="slide",
    )(
        place,
        *all_tiles,
        long_gain[None, :],
        jnp.transpose(long_query),
        jnp.transpose(long_key),
        jnp.transpose(long_value),
        long_out,
    )
    terms = deal(terms, "fsdp")
    summed = terms[0].astype(F32)
    for step in range(1, size):
        summed = summed + terms[step].astype(F32)
    return (residual + summed).astype(BF16)


def solution(mesh):
    return jax.shard_map(
        local,
        mesh=mesh,
        in_specs=(
            P(("group", "seq", "fsdp"), None, None),
            P(),
            P("fsdp", None),
            P("fsdp", None),
            P("fsdp", None),
            P("fsdp", None),
            P("fsdp", None),
            P(),
            P(None, "fsdp"),
            P(None, "fsdp"),
            P(None, "fsdp"),
            P("fsdp", None),
            P(("group", "seq", "fsdp")),
            P(("group", "seq", "fsdp")),
        ),
        out_specs=P(("group", "seq"), "fsdp"),
        check_vma=False,
    )
```

```python
import functools
import math

import jax
import jax.numpy as jnp
from jax import lax
from jax.experimental import pallas as pl
from jax.experimental.pallas import tpu as pltpu
from jax.sharding import PartitionSpec as P

VHD = 64
HEADS = 16
DILATION_STEP = 4
EPSILON = 1e-06
LANES = 128


BF16 = jnp.bfloat16
F32 = jnp.float32


def other(index, step, size):
    return index ^ step if size & (size - 1) == 0 else (index + step) % size


def source(index, step, size):
    return index ^ step if size & (size - 1) == 0 else (index + size - step) % size


def swap(array, axis, step):
    size = lax.axis_size(axis)
    return lax.ppermute(array, axis, [(i, other(i, step, size)) for i in range(size)])


def spread(array, axis):
    return [array] + [swap(array, axis, step) for step in range(1, lax.axis_size(axis))]


def deal(arrays, axis):
    return [arrays[0]] + [swap(arrays[step], axis, step) for step in range(1, len(arrays))]


def normalise(rows, gain):
    average = jnp.mean(rows, axis=-1, keepdims=True)
    centred = rows - average
    variance = jnp.mean(centred * centred, axis=-1, keepdims=True)
    return (centred * lax.rsqrt(variance + EPSILON) * gain).astype(BF16)


def contract(left, right, left_axis, right_axis):
    return lax.dot_general(
        left, right, (((left_axis,), (right_axis,)), ((), ())), preferred_element_type=F32
    )


def in_hbm(array):
    return pltpu.with_memory_space_constraint(array, pltpu.HBM)


def call(body, outs, scratch=(), name=None, limit=1 << 23, specs=()):
    smem, vmem = pl.BlockSpec(memory_space=pltpu.SMEM), pl.BlockSpec(memory_space=pltpu.VMEM)

    def run(place, *arrays):
        last = len(arrays) - len(specs)
        return pl.pallas_call(
            body,
            out_shape=outs,
            in_specs=[smem] + [vmem] * last + [pl.BlockSpec(memory_space=m) for m in specs],
            out_specs=jax.tree.map(lambda _: vmem, outs),
            scratch_shapes=list(scratch),
            compiler_params=pltpu.CompilerParams(vmem_limit_bytes=limit),
            name=name,
        )(place, *arrays)

    return run


def head_kernel(tokens, out):
    for tile in range(tokens.shape[0]):
        out[tile : tile + 1, :] = tokens[tile, 0:1, :]


def notes_kernel(size, place, order, counts, after, out, rows):
    me = place[0] % size
    tiles = order.shape[0]
    lane = lax.broadcasted_iota(jnp.int32, (1, LANES), 1)
    rows[...] = jnp.zeros_like(rows)
    for tile in range(tiles):
        spot = order[tile]
        present = (counts[0] > tile).astype(jnp.int32)
        high = jnp.where(lane == 0, spot // 256, 0)
        low = jnp.where(lane == 1, spot % 256, 0)
        notes = high + low + jnp.where(lane == 2, present, 0)
        rows[me, tile : tile + 1, :] = notes.astype(F32)
    out[...] = rows[...].reshape(size * tiles, LANES).astype(BF16)


def query_kernel(size, place, *refs):
    heads_in, (gain, weight, out, first, rows, blocks) = refs[:size], refs[size:]
    me = place[0] % size
    tiles, width = heads_in[0].shape
    mine = weight.shape[0]
    for step in range(size):
        rows[source(me, step, size)] = heads_in[step][...].astype(F32)
    full = rows[...].reshape(size * tiles, width)
    for block in range(size):
        blocks[block] = full[:, block * mine : (block + 1) * mine]
    first[...] = blocks[me]
    normed = normalise(full, gain[...]).astype(F32)
    for block in range(size):
        blocks[block] = normed[:, block * mine : (block + 1) * mine]
    out[...] = contract(blocks[me].astype(BF16), weight[...], 1, 0).astype(BF16)


def grouped(shape, axis, span):
    return lax.broadcasted_iota(jnp.int32, shape, axis) // span


def own_head(shape, heads):
    row = lax.broadcasted_iota(jnp.int32, shape, 0) % heads
    return row == grouped(shape, 1, VHD)


def fold_kernel(size, heads, place, *refs):
    parts, weight, outs, folded = refs[:size], refs[size], refs[size + 1 : -1], refs[-1]
    me = place[0] % size
    total = parts[0][...].astype(F32)
    for step in range(1, size):
        total = total + parts[step][...].astype(F32)
    count, width = total.shape
    spots = (count * heads, count)
    repeat = grouped(spots, 0, heads) == lax.broadcasted_iota(jnp.int32, spots, 1)
    repeated = contract(repeat.astype(F32).astype(BF16), total.astype(BF16), 1, 0)
    blocked = jnp.where(own_head(repeated.shape, heads), repeated, 0.0).astype(BF16)
    folded[...] = contract(blocked, weight[...], 1, 1).astype(BF16).reshape(folded.shape)
    for step in range(size):
        outs[step][...] = folded[other(me, step, size)]


def cut_kernel(size, steps, place, weight, after, *refs):
    outs, blocks = refs[:-1], refs[-1]
    me = place[0] % size
    mine = weight.shape[1] // size
    for block in range(size):
        blocks[block] = weight[:, block * mine : (block + 1) * mine]
    for out, step in zip(outs, steps):
        out[...] = blocks[other(me, step, size)]


def token_kernel(size, heads, place, *refs):
    parts, normed, outs, (blocks, folded) = (
        refs[:size],
        refs[size],
        refs[size + 1 : -2],
        refs[-2:],
    )
    me = place[0] % size
    rows = parts[0].shape[1]
    for step in range(size):
        blocks[source(me, step, size)] = parts[step][...]
    for block in range(size):
        folded[:, block * rows : (block + 1) * rows] = blocks[block]
    tiles, patches, width = normed.shape
    tokens = normed[...].reshape(tiles * patches, width)
    scores = contract(folded[...], tokens, 1, 1) / math.sqrt(VHD)
    same = grouped(scores.shape, 0, heads) == grouped(scores.shape, 1, patches)
    lifted = jnp.where(same, jnp.exp(scores), 0.0)
    probs = (lifted / jnp.sum(lifted, axis=-1, keepdims=True)).astype(BF16)
    mixed = contract(probs, tokens, 1, 0).astype(BF16)
    for block in range(size):
        blocks[block] = mixed[:, block * rows : (block + 1) * rows]
    for step in range(size):
        outs[step][...] = blocks[other(me, step, size)]


def value_kernel(size, heads, place, *refs):
    parts, (weight, out, mixed) = refs[:size], refs[size:]
    me = place[0] % size
    for step in range(size):
        mixed[source(me, step, size)] = parts[step][...]
    rows = mixed[...].reshape(size * parts[0].shape[0], parts[0].shape[1])
    product = contract(rows, weight[...], 1, 0)
    kept = jnp.where(own_head(product.shape, heads), product, 0.0).astype(BF16)
    spots = (out.shape[0], product.shape[0])
    collect = lax.broadcasted_iota(jnp.int32, spots, 0) == grouped(spots, 1, heads)
    out[...] = contract(collect.astype(F32).astype(BF16), kept, 1, 0).astype(BF16)


def embed_kernel(size, place, *refs):
    parts, blocks, (first, project, notes, out, weight) = (
        refs[:size],
        refs[size : 2 * size],
        refs[2 * size :],
    )
    me = place[0] % size
    total = parts[0][...].astype(F32)
    for step in range(1, size):
        total = total + parts[step][...].astype(F32)
    pooled = total.astype(BF16)
    depth = blocks[0].shape[0]
    for step in range(size):
        start = pl.multiple_of(source(me, step, size) * depth, 16)
        weight[pl.ds(start, depth), :] = blocks[step][...]
    class_row = (first[...] + contract(pooled, weight[...], 1, 0)).astype(BF16)
    width = project.shape[1]
    out[:, :width] = contract(class_row, project[...], 1, 0).astype(BF16)
    out[:, width:] = notes[...]


def gather_kernel(*refs):
    parts, out = refs[1:-1], refs[-1]
    total = parts[0][...].astype(F32)
    for part in parts[1:]:
        total = total + part[...].astype(F32)
    width = total.shape[1] - LANES
    there = total[:, width + 2 : width + 3] > 0
    out[:, :width] = jnp.where(there, total[:, :width], 0.0).astype(BF16)
    out[:, width:] = total[:, width:].astype(BF16)


def slide_kernel(size, seq_size, place, *refs):
    parts = refs[:seq_size]
    gain, w_query, w_key, w_value, w_out = refs[seq_size : seq_size + 5]
    outs, (long_normed, blocks) = refs[seq_size + 5 : -2], refs[-2:]
    me, seq = place[0] % size, place[0] // size
    rows = parts[0].shape[0]
    model = gain.shape[1]
    width = w_query.shape[0]
    total = rows * seq_size
    segment = total // 4
    tiles = jnp.concatenate([part[...].astype(F32) for part in parts], axis=0)
    notes = tiles[:, model:]
    order = notes[:, 0:1] * 256.0 + notes[:, 1:2]
    spots = lax.broadcasted_iota(jnp.int32, (total, total), 1).astype(F32)
    picker = jnp.where(order == spots, 1.0, 0.0)
    picked = contract(picker.astype(BF16), tiles.astype(BF16), 0, 0)
    long_normed[...] = normalise(picked[:, :model], gain[...]).astype(F32)
    normed = long_normed[...].astype(BF16)
    mine = pl.ds(pl.multiple_of(seq * rows, 8), rows)
    queries = contract(long_normed[mine, :].astype(BF16), w_query[...], 1, 1).astype(BF16)
    keys = contract(normed, w_key[...], 1, 1).astype(BF16)
    values = contract(normed, w_value[...], 1, 1).astype(BF16)
    here = jnp.sum(jnp.where(order == spots, notes[:, 2:3], 0.0), axis=0, keepdims=True)
    head_size = model // HEADS
    count = width // head_size
    shape = (count, rows, width)
    owner = lax.broadcasted_iota(jnp.int32, shape, 2) // head_size
    own = owner == lax.broadcasted_iota(jnp.int32, shape, 0)
    blocked = jnp.where(own, jnp.broadcast_to(queries.astype(F32)[None], shape), 0.0)
    blocked = blocked.reshape(count * rows, width).astype(BF16)
    scores = contract(blocked, keys, 1, 1) / math.sqrt(head_size)
    line = lax.broadcasted_iota(jnp.int32, (count * rows, total), 0)
    asking = seq * rows + line % rows
    shift = (me * count + line // rows) % DILATION_STEP
    key_at = lax.broadcasted_iota(jnp.int32, (count * rows, total), 1)
    allowed = (here > 0) | (asking == key_at)
    near = (asking // segment == key_at // segment) & allowed
    far = (asking % DILATION_STEP == shift) & (key_at % DILATION_STEP == shift) & allowed
    times = jnp.where(near, 1.0, 0.0) + jnp.where(far, 1.0, 0.0)
    lifted = jnp.where(times > 0, jnp.exp(scores), 0.0)
    bottom = jnp.sum(lifted * times, axis=-1, keepdims=True)
    weights = (lifted.astype(BF16).astype(F32) * times).astype(BF16)
    mixed = (contract(weights, values, 1, 0) / bottom).reshape(shape)
    attended = jnp.sum(jnp.where(own, mixed, 0.0), axis=0).astype(BF16)
    terms = contract(attended, w_out[...], 1, 0)
    for block in range(size):
        blocks[block] = terms[:, block * width : (block + 1) * width]
    for step in range(size):
        outs[step][...] = blocks[other(me, step, size)].astype(BF16)
    long_normed[...] = picked[:, :model]
    at_home = long_normed[mine, :]
    for block in range(size):
        blocks[block] = at_home[:, block * width : (block + 1) * width]
    outs[size][...] = blocks[me]


def local(
    tile_patches,
    vit_gain,
    w_query,
    w_key,
    w_value,
    w_out,
    w_proj,
    long_gain,
    long_query,
    long_key,
    long_value,
    long_out,
    seq_order,
    counts,
):
    size = lax.axis_size("fsdp")
    seq_size = lax.axis_size("seq")
    me = lax.axis_index("fsdp")
    place = (lax.axis_index("seq") * size + me).astype(jnp.int32).reshape(1)
    tiles, patches, width = tile_patches.shape
    vit_width = w_key.shape[1]
    heads = vit_width // VHD
    rows = w_key.shape[0]
    model = w_proj.shape[1]
    depth = w_out.shape[0]
    count = tiles * size

    head_row = pl.pallas_call(
        head_kernel,
        out_shape=jax.ShapeDtypeStruct((tiles, width), BF16),
        grid=(1,),
        in_specs=[pl.BlockSpec((tiles, 8, width), lambda i: (0, 0, 0))],
        out_specs=pl.BlockSpec(memory_space=pltpu.VMEM),
        compiler_params=pltpu.CompilerParams(vmem_limit_bytes=1 << 20),
        name="head",
    )(in_hbm(tile_patches))
    head_rows = spread(head_row, "fsdp")
    notes = call(
        functools.partial(notes_kernel, size),
        jax.ShapeDtypeStruct((count, LANES), BF16),
        [pltpu.VMEM((size, tiles, LANES), F32)],
        name="notes",
        specs=[pltpu.SMEM, pltpu.SMEM, pl.ANY],
    )(place, seq_order, counts, head_row)

    def cut(steps, after):
        blocks = call(
            functools.partial(cut_kernel, size, steps),
            [jax.ShapeDtypeStruct((depth, width // size), BF16)] * len(steps),
            [pltpu.VMEM((size, depth, width // size), BF16)],
            name="cut",
            specs=[pl.ANY],
        )(place, w_out, after)
        return {
            step: swap(block, "fsdp", step) if step else block
            for step, block in zip(steps, blocks)
        }

    out_blocks = cut(range(1, size, 2), head_row)

    normed = normalise(tile_patches.astype(F32), vit_gain)

    gain_row = vit_gain[None, :]
    query_part, first = call(
        functools.partial(query_kernel, size),
        [
            jax.ShapeDtypeStruct((count, vit_width), BF16),
            jax.ShapeDtypeStruct((count, rows), F32),
        ],
        [pltpu.VMEM((size, tiles, width), F32), pltpu.VMEM((size, count, rows), F32)],
        name="query",
    )(place, *head_rows, gain_row, w_query)
    query_parts = spread(query_part, "fsdp")

    block = jax.ShapeDtypeStruct((tiles * heads, rows), BF16)
    folded = call(
        functools.partial(fold_kernel, size, heads),
        [block] * size,
        [pltpu.VMEM((size, tiles * heads, rows), BF16)],
        name="fold",
    )(place, *query_parts, w_key)
    out_blocks |= cut(range(0, size, 2), folded[0])
    folded = deal(folded, "fsdp")

    mixed = call(
        functools.partial(token_kernel, size, heads),
        [block] * size,
        [pltpu.VMEM((size, tiles * heads, rows), BF16), pltpu.VMEM((tiles * heads, width), BF16)],
        name="tokens",
    )(place, *folded, normed)
    mixed = deal(mixed, "fsdp")

    pooled_part = call(
        functools.partial(value_kernel, size, heads),
        jax.ShapeDtypeStruct((count, vit_width), BF16),
        [pltpu.VMEM((size, tiles * heads, rows), BF16)],
        name="value",
    )(place, *mixed, w_value)
    pooled_parts = spread(pooled_part, "fsdp")

    embed_part = call(
        functools.partial(embed_kernel, size),
        jax.ShapeDtypeStruct((count, model + LANES), BF16),
        [pltpu.VMEM((vit_width, width // size), BF16)],
        name="embed",
    )(place, *pooled_parts, *(out_blocks[step] for step in range(size)), first, w_proj, notes)
    embed_parts = spread(embed_part, "fsdp")

    group_tiles = call(
        gather_kernel, jax.ShapeDtypeStruct((count, model + LANES), BF16), name="gather"
    )(place, *embed_parts)
    all_tiles = spread(group_tiles, "seq")

    head_width = long_query.shape[1]
    outs = [jax.ShapeDtypeStruct((count, head_width), BF16)] * size + [
        jax.ShapeDtypeStruct((count, head_width), F32)
    ]
    *terms, residual = call(
        functools.partial(slide_kernel, size, seq_size),
        outs,
        [
            pltpu.VMEM((count * seq_size, model), F32),
            pltpu.VMEM((size, count, head_width), F32),
        ],
        name="slide",
    )(
        place,
        *all_tiles,
        long_gain[None, :],
        jnp.transpose(long_query),
        jnp.transpose(long_key),
        jnp.transpose(long_value),
        long_out,
    )
    terms = deal(terms, "fsdp")
    summed = terms[0].astype(F32)
    for step in range(1, size):
        summed = summed + terms[step].astype(F32)
    return (residual + summed).astype(BF16)


def solution(mesh):
    return jax.shard_map(
        local,
        mesh=mesh,
        in_specs=(
            P(("group", "seq", "fsdp"), None, None),
            P(),
            P("fsdp", None),
            P("fsdp", None),
            P("fsdp", None),
            P("fsdp", None),
            P("fsdp", None),
            P(),
            P(None, "fsdp"),
            P(None, "fsdp"),
            P(None, "fsdp"),
            P("fsdp", None),
            P(("group", "seq", "fsdp")),
            P(("group", "seq", "fsdp")),
        ),
        out_specs=P(("group", "seq"), "fsdp"),
        check_vma=False,
    )
```

```python
import functools
import math

import jax
import jax.numpy as jnp
from jax import lax
from jax.experimental import pallas as pl
from jax.experimental.pallas import tpu as pltpu
from jax.sharding import PartitionSpec as P


VHD = 64
HEADS = 16
DILATION_STEP = 4
EPSILON = 1e-06
LANES = 128


BF16 = jnp.bfloat16
F32 = jnp.float32


def other(index, step, size):
    return index ^ step if size & (size - 1) == 0 else (index + step) % size


def source(index, step, size):
    return index ^ step if size & (size - 1) == 0 else (index + size - step) % size


def swap(array, axis, step):
    size = lax.axis_size(axis)
    return lax.ppermute(array, axis, [(i, other(i, step, size)) for i in range(size)])


def spread(array, axis):
    return [array] + [swap(array, axis, step) for step in range(1, lax.axis_size(axis))]


def deal(arrays, axis):
    return [arrays[0]] + [swap(arrays[step], axis, step) for step in range(1, len(arrays))]


def normalise(rows, gain):
    average = jnp.mean(rows, axis=-1, keepdims=True)
    centred = rows - average
    variance = jnp.mean(centred * centred, axis=-1, keepdims=True)
    return (centred * lax.rsqrt(variance + EPSILON) * gain).astype(BF16)


def contract(left, right, left_axis, right_axis):
    return lax.dot_general(
        left, right, (((left_axis,), (right_axis,)), ((), ())), preferred_element_type=F32
    )


def in_hbm(array):
    return pltpu.with_memory_space_constraint(array, pltpu.HBM)


def call(body, outs, scratch=(), limit=1 << 23, specs=()):
    smem, vmem = pl.BlockSpec(memory_space=pltpu.SMEM), pl.BlockSpec(memory_space=pltpu.VMEM)

    def run(place, *arrays):
        last = len(arrays) - len(specs)
        return pl.pallas_call(
            body,
            out_shape=outs,
            in_specs=[smem] + [vmem] * last + [pl.BlockSpec(memory_space=m) for m in specs],
            out_specs=jax.tree.map(lambda _: vmem, outs),
            scratch_shapes=list(scratch),
            compiler_params=pltpu.CompilerParams(vmem_limit_bytes=limit),
        )(place, *arrays)

    return run


def head_kernel(tokens, out):
    for tile in range(tokens.shape[0]):
        out[tile : tile + 1, :] = tokens[tile, 0:1, :]


def notes_kernel(size, place, order, counts, after, out, rows):
    me = place[0] % size
    tiles = order.shape[0]
    lane = lax.broadcasted_iota(jnp.int32, (1, LANES), 1)
    rows[...] = jnp.zeros_like(rows)
    for tile in range(tiles):
        spot = order[tile]
        present = (counts[0] > tile).astype(jnp.int32)
        high = jnp.where(lane == 0, spot // 256, 0)
        low = jnp.where(lane == 1, spot % 256, 0)
        notes = high + low + jnp.where(lane == 2, present, 0)
        rows[me, tile : tile + 1, :] = notes.astype(F32)
    out[...] = rows[...].reshape(size * tiles, LANES).astype(BF16)


def query_kernel(size, place, *refs):
    heads_in, (gain, weight, out, first, rows, blocks) = refs[:size], refs[size:]
    me = place[0] % size
    tiles, width = heads_in[0].shape
    mine = weight.shape[0]
    for step in range(size):
        rows[source(me, step, size)] = heads_in[step][...].astype(F32)
    full = rows[...].reshape(size * tiles, width)
    for block in range(size):
        blocks[block] = full[:, block * mine : (block + 1) * mine]
    first[...] = blocks[me]
    normed = normalise(full, gain[...]).astype(F32)
    for block in range(size):
        blocks[block] = normed[:, block * mine : (block + 1) * mine]
    out[...] = contract(blocks[me].astype(BF16), weight[...], 1, 0).astype(BF16)


def grouped(shape, axis, span):
    return lax.broadcasted_iota(jnp.int32, shape, axis) // span


def own_head(shape, heads):
    row = lax.broadcasted_iota(jnp.int32, shape, 0) % heads
    return row == grouped(shape, 1, VHD)


def fold_kernel(size, heads, place, *refs):
    parts, weight, outs, folded = refs[:size], refs[size], refs[size + 1 : -1], refs[-1]
    me = place[0] % size
    total = parts[0][...].astype(F32)
    for step in range(1, size):
        total = total + parts[step][...].astype(F32)
    count, _ = total.shape
    spots = (count * heads, count)
    repeat = grouped(spots, 0, heads) == lax.broadcasted_iota(jnp.int32, spots, 1)
    repeated = contract(repeat.astype(F32).astype(BF16), total.astype(BF16), 1, 0)
    blocked = jnp.where(own_head(repeated.shape, heads), repeated, 0.0).astype(BF16)
    folded[...] = contract(blocked, weight[...], 1, 1).astype(BF16).reshape(folded.shape)
    for step in range(size):
        outs[step][...] = folded[other(me, step, size)]


def cut_kernel(size, place, weight, after, *refs):
    outs, blocks = refs[:-1], refs[-1]
    me = place[0] % size
    mine = weight.shape[1] // size
    for block in range(size):
        blocks[block] = weight[:, block * mine : (block + 1) * mine]
    for step in range(size):
        outs[step][...] = blocks[other(me, step, size)]


def token_kernel(size, heads, place, *refs):
    parts, normed, outs, (blocks, folded) = (
        refs[:size],
        refs[size],
        refs[size + 1 : -2],
        refs[-2:],
    )
    me = place[0] % size
    rows = parts[0].shape[1]
    for step in range(size):
        blocks[source(me, step, size)] = parts[step][...]
    for block in range(size):
        folded[:, block * rows : (block + 1) * rows] = blocks[block]
    tiles, patches, width = normed.shape
    tokens = normed[...].reshape(tiles * patches, width)
    scores = contract(folded[...], tokens, 1, 1) / math.sqrt(VHD)
    same = grouped(scores.shape, 0, heads) == grouped(scores.shape, 1, patches)
    lifted = jnp.where(same, jnp.exp(scores), 0.0)
    probs = (lifted / jnp.sum(lifted, axis=-1, keepdims=True)).astype(BF16)
    mixed = contract(probs, tokens, 1, 0).astype(BF16)
    for block in range(size):
        blocks[block] = mixed[:, block * rows : (block + 1) * rows]
    for step in range(size):
        outs[step][...] = blocks[other(me, step, size)]


def value_kernel(size, heads, place, *refs):
    parts, (weight, out, mixed) = refs[:size], refs[size:]
    me = place[0] % size
    for step in range(size):
        mixed[source(me, step, size)] = parts[step][...]
    rows = mixed[...].reshape(size * parts[0].shape[0], parts[0].shape[1])
    product = contract(rows, weight[...], 1, 0)
    kept = jnp.where(own_head(product.shape, heads), product, 0.0).astype(BF16)
    spots = (out.shape[0], product.shape[0])
    collect = lax.broadcasted_iota(jnp.int32, spots, 0) == grouped(spots, 1, heads)
    out[...] = contract(collect.astype(F32).astype(BF16), kept, 1, 0).astype(BF16)


def embed_kernel(size, place, *refs):
    parts, blocks, (first, project, notes, out, weight) = (
        refs[:size],
        refs[size : 2 * size],
        refs[2 * size :],
    )
    me = place[0] % size
    total = parts[0][...].astype(F32)
    for step in range(1, size):
        total = total + parts[step][...].astype(F32)
    pooled = total.astype(BF16)
    depth = blocks[0].shape[0]
    for step in range(size):
        start = pl.multiple_of(source(me, step, size) * depth, 16)
        weight[pl.ds(start, depth), :] = blocks[step][...]
    class_row = (first[...] + contract(pooled, weight[...], 1, 0)).astype(BF16)
    width = project.shape[1]
    out[:, :width] = contract(class_row, project[...], 1, 0).astype(BF16)
    out[:, width:] = notes[...]


def gather_kernel(*refs):
    parts, out = refs[1:-1], refs[-1]
    total = parts[0][...].astype(F32)
    for part in parts[1:]:
        total = total + part[...].astype(F32)
    width = total.shape[1] - LANES
    there = total[:, width + 2 : width + 3] > 0
    out[:, :width] = jnp.where(there, total[:, :width], 0.0).astype(BF16)
    out[:, width:] = total[:, width:].astype(BF16)


def along_lanes(column):
    shape = (column.shape[0], column.shape[0])
    here = lax.broadcasted_iota(jnp.int32, shape, 0) == lax.broadcasted_iota(jnp.int32, shape, 1)
    return jnp.sum(jnp.where(here, column, 0.0), axis=0, keepdims=True)


def slide_kernel(size, seq_size, place, *refs):
    parts = refs[:seq_size]
    gain, w_query, w_key, w_value = refs[seq_size : seq_size + 4]
    w_out, outs = refs[seq_size + 4 : seq_size + 4 + size], refs[seq_size + 4 + size :]
    me, seq = place[0] % size, place[0] // size
    rows = parts[0].shape[0]
    model = gain.shape[1]
    width = w_query.shape[0]
    total = rows * seq_size
    segment = total // 4
    tiles = jnp.concatenate([part[...].astype(F32) for part in parts], axis=0)
    notes = tiles[:, model:]
    position = along_lanes(notes[:, 0:1] * 256.0 + notes[:, 1:2]).astype(jnp.int32)
    here = along_lanes(notes[:, 2:3])
    normed = normalise(tiles[:, :model], gain[...])
    keys = contract(normed, w_key[...], 1, 1).astype(BF16)
    values = contract(normed, w_value[...], 1, 1).astype(BF16)
    asked = seq * rows + lax.broadcasted_iota(jnp.int32, (rows, total), 0)
    picker = jnp.where(asked == position, 1.0, 0.0).astype(BF16)
    mine = contract(picker, normed, 1, 0).astype(BF16)
    queries = contract(mine, w_query[...], 1, 1).astype(BF16).astype(F32)
    head_size = model // HEADS
    count = width // head_size
    shape = (count, rows, width)
    own = grouped(shape, 2, head_size) == lax.broadcasted_iota(jnp.int32, shape, 0)
    blocked = jnp.where(own, jnp.broadcast_to(queries[None], shape), 0.0)
    blocked = blocked.reshape(count * rows, width).astype(BF16)
    scores = contract(blocked, keys, 1, 1) / math.sqrt(head_size)
    line = lax.broadcasted_iota(jnp.int32, (count * rows, total), 0)
    asking = seq * rows + line % rows
    shift = (me * count + line // rows) % DILATION_STEP
    allowed = (here > 0) | (asking == position)
    near = (asking // segment == position // segment) & allowed
    far = (asking % DILATION_STEP == shift) & (position % DILATION_STEP == shift) & allowed
    times = jnp.where(near, 1.0, 0.0) + jnp.where(far, 1.0, 0.0)
    lifted = jnp.where(times > 0, jnp.exp(scores), 0.0)
    bottom = jnp.sum(lifted * times, axis=-1, keepdims=True)
    weights = (lifted.astype(BF16).astype(F32) * times).astype(BF16)
    mixed = (contract(weights, values, 1, 0) / bottom).reshape(shape)
    attended = jnp.sum(jnp.where(own, mixed, 0.0), axis=0).astype(BF16)
    for step in range(size):
        outs[step][...] = contract(attended, w_out[step][...], 1, 0).astype(BF16)


def residual_kernel(size, seq_size, place, *refs):
    parts, (after, out, blocks) = refs[:seq_size], refs[seq_size:]
    me, seq = place[0] % size, place[0] // size
    rows, width = out.shape
    total = rows * seq_size
    tiles = jnp.concatenate([part[...].astype(F32) for part in parts], axis=0)
    notes = tiles[:, size * width :]
    position = along_lanes(notes[:, 0:1] * 256.0 + notes[:, 1:2]).astype(jnp.int32)
    asked = seq * rows + lax.broadcasted_iota(jnp.int32, (rows, total), 0)
    picker = jnp.where(asked == position, 1.0, 0.0).astype(BF16)
    mine = contract(picker, tiles[:, : size * width].astype(BF16), 1, 0)
    for block in range(size):
        blocks[block] = mine[:, block * width : (block + 1) * width]
    out[...] = blocks[me]


def local(
    tile_patches,
    vit_gain,
    w_query,
    w_key,
    w_value,
    w_out,
    w_proj,
    long_gain,
    long_query,
    long_key,
    long_value,
    long_out,
    seq_order,
    counts,
):
    size = lax.axis_size("fsdp")
    seq_size = lax.axis_size("seq")
    me = lax.axis_index("fsdp")
    place = (lax.axis_index("seq") * size + me).astype(jnp.int32).reshape(1)
    tiles, _, width = tile_patches.shape
    vit_width = w_key.shape[1]
    heads = vit_width // VHD
    rows = w_key.shape[0]
    model = w_proj.shape[1]
    count = tiles * size

    head_row = pl.pallas_call(
        head_kernel,
        out_shape=jax.ShapeDtypeStruct((tiles, width), BF16),
        grid=(1,),
        in_specs=[pl.BlockSpec((tiles, 8, width), lambda i: (0, 0, 0))],
        out_specs=pl.BlockSpec(memory_space=pltpu.VMEM),
        compiler_params=pltpu.CompilerParams(vmem_limit_bytes=1 << 20),
        name="head",
    )(in_hbm(tile_patches))
    head_rows = spread(head_row, "fsdp")
    notes = call(
        functools.partial(notes_kernel, size),
        jax.ShapeDtypeStruct((count, LANES), BF16),
        [pltpu.VMEM((size, tiles, LANES), F32)],
        specs=[pltpu.SMEM, pltpu.SMEM, pl.ANY],
    )(place, seq_order, counts, head_row)

    def cut(weight, after):
        shape = (weight.shape[0], weight.shape[1] // size)
        return call(
            functools.partial(cut_kernel, size),
            [jax.ShapeDtypeStruct(shape, BF16)] * size,
            [pltpu.VMEM((size, *shape), BF16)],
            specs=[pl.ANY],
        )(place, weight, after)

    out_blocks = deal(cut(w_out, head_row), "fsdp")

    normed = normalise(tile_patches.astype(F32), vit_gain)

    gain_row = vit_gain[None, :]
    query_part, first = call(
        functools.partial(query_kernel, size),
        [
            jax.ShapeDtypeStruct((count, vit_width), BF16),
            jax.ShapeDtypeStruct((count, rows), F32),
        ],
        [pltpu.VMEM((size, tiles, width), F32), pltpu.VMEM((size, count, rows), F32)],
    )(place, *head_rows, gain_row, w_query)
    query_parts = spread(query_part, "fsdp")

    block = jax.ShapeDtypeStruct((tiles * heads, rows), BF16)
    folded = call(
        functools.partial(fold_kernel, size, heads),
        [block] * size,
        [pltpu.VMEM((size, tiles * heads, rows), BF16)],
    )(place, *query_parts, w_key)
    folded = deal(folded, "fsdp")

    mixed = call(
        functools.partial(token_kernel, size, heads),
        [block] * size,
        [pltpu.VMEM((size, tiles * heads, rows), BF16), pltpu.VMEM((tiles * heads, width), BF16)],
    )(place, *folded, normed)
    mixed = deal(mixed, "fsdp")

    pooled_part = call(
        functools.partial(value_kernel, size, heads),
        jax.ShapeDtypeStruct((count, vit_width), BF16),
        [pltpu.VMEM((size, tiles * heads, rows), BF16)],
    )(place, *mixed, w_value)
    pooled_parts = spread(pooled_part, "fsdp")

    embed_part = call(
        functools.partial(embed_kernel, size),
        jax.ShapeDtypeStruct((count, model + LANES), BF16),
        [pltpu.VMEM((vit_width, width // size), BF16)],
    )(place, *pooled_parts, *out_blocks, first, w_proj, notes)
    embed_parts = spread(embed_part, "fsdp")

    group_tiles = call(
        gather_kernel, jax.ShapeDtypeStruct((count, model + LANES), BF16)
    )(place, *embed_parts)
    all_tiles = spread(group_tiles, "seq")

    head_width = long_query.shape[1]
    long_blocks = cut(long_out, pooled_part)
    block = jax.ShapeDtypeStruct((count, head_width), BF16)
    terms = call(functools.partial(slide_kernel, size, seq_size), [block] * size)(
        place,
        *all_tiles,
        long_gain[None, :],
        jnp.transpose(long_query),
        jnp.transpose(long_key),
        jnp.transpose(long_value),
        *long_blocks,
    )
    residual = call(
        functools.partial(residual_kernel, size, seq_size),
        jax.ShapeDtypeStruct((count, head_width), F32),
        [pltpu.VMEM((size, count, head_width), F32)],
        specs=[pl.ANY],
    )(place, *all_tiles, terms[0])
    terms = deal(terms, "fsdp")
    summed = terms[0].astype(F32)
    for step in range(1, size):
        summed = summed + terms[step].astype(F32)
    return (residual + summed).astype(BF16)


def solution(mesh):
    return jax.shard_map(
        local,
        mesh=mesh,
        in_specs=(
            P(("group", "seq", "fsdp"), None, None),
            P(),
            P("fsdp", None),
            P("fsdp", None),
            P("fsdp", None),
            P("fsdp", None),
            P("fsdp", None),
            P(),
            P(None, "fsdp"),
            P(None, "fsdp"),
            P(None, "fsdp"),
            P("fsdp", None),
            P(("group", "seq", "fsdp")),
            P(("group", "seq", "fsdp")),
        ),
        out_specs=P(("group", "seq"), "fsdp"),
        check_vma=False,
    )
```

```python
import functools
import math

import jax
import jax.numpy as jnp
from jax import lax
from jax.experimental import pallas as pl
from jax.experimental.pallas import tpu as pltpu
from jax.sharding import PartitionSpec as P


VHD = 64
HEADS = 16
DILATION_STEP = 4
EPSILON = 1e-06
LANES = 128


BF16 = jnp.bfloat16
F32 = jnp.float32


def other(index, step, size):
    return index ^ step if size & (size - 1) == 0 else (index + step) % size


def source(index, step, size):
    return index ^ step if size & (size - 1) == 0 else (index + size - step) % size


def swap(array, axis, step):
    size = lax.axis_size(axis)
    return lax.ppermute(array, axis, [(i, other(i, step, size)) for i in range(size)])


def spread(array, axis):
    return [array] + [swap(array, axis, step) for step in range(1, lax.axis_size(axis))]


def rows_of_all(array):
    size, seq_size = lax.axis_size("fsdp"), lax.axis_size("seq")
    if size % 2 or seq_size & (seq_size - 1) or seq_size < 4:
        return spread(array, "seq")
    direct = [swap(array, "seq", step) for step in range(3, seq_size)]
    pairs = [
        (row * size + place, (row ^ (1 + place % 2)) * size + place)
        for row in range(seq_size)
        for place in range(size)
    ]
    near = lax.ppermute(array, ("seq", "fsdp"), pairs)
    return [array, near, swap(near, "fsdp", 1), *direct]


def deal(arrays, axis):
    return [arrays[0]] + [swap(arrays[step], axis, step) for step in range(1, len(arrays))]


def normalise(rows, gain):
    average = jnp.mean(rows, axis=-1, keepdims=True)
    centred = rows - average
    variance = jnp.mean(centred * centred, axis=-1, keepdims=True)
    return (centred * lax.rsqrt(variance + EPSILON) * gain).astype(BF16)


def contract(left, right, left_axis, right_axis):
    return lax.dot_general(
        left, right, (((left_axis,), (right_axis,)), ((), ())), preferred_element_type=F32
    )


def in_hbm(array):
    return pltpu.with_memory_space_constraint(array, pltpu.HBM)


def call(body, outs, scratch=(), limit=1 << 23, specs=()):
    smem, vmem = pl.BlockSpec(memory_space=pltpu.SMEM), pl.BlockSpec(memory_space=pltpu.VMEM)

    def run(place, *arrays):
        last = len(arrays) - len(specs)
        return pl.pallas_call(
            body,
            out_shape=outs,
            in_specs=[smem] + [vmem] * last + [pl.BlockSpec(memory_space=m) for m in specs],
            out_specs=jax.tree.map(lambda _: vmem, outs),
            scratch_shapes=list(scratch),
            compiler_params=pltpu.CompilerParams(vmem_limit_bytes=limit),
        )(place, *arrays)

    return run


def head_kernel(tokens, out):
    for tile in range(tokens.shape[0]):
        out[tile : tile + 1, :] = tokens[tile, 0:1, :]


def notes_kernel(size, place, order, counts, after, out, rows):
    me = place[0] % size
    tiles = order.shape[0]
    lane = lax.broadcasted_iota(jnp.int32, (1, LANES), 1)
    rows[...] = jnp.zeros_like(rows)
    for tile in range(tiles):
        spot = order[tile]
        present = (counts[0] > tile).astype(jnp.int32)
        high = jnp.where(lane == 0, spot // 256, 0)
        low = jnp.where(lane == 1, spot % 256, 0)
        notes = high + low + jnp.where(lane == 2, present, 0)
        rows[me, tile : tile + 1, :] = notes.astype(F32)
    out[...] = rows[...].reshape(size * tiles, LANES).astype(BF16)


def query_kernel(size, place, *refs):
    heads_in, (gain, weight, out, first, rows, blocks) = refs[:size], refs[size:]
    me = place[0] % size
    tiles, width = heads_in[0].shape
    mine = weight.shape[0]
    for step in range(size):
        rows[source(me, step, size)] = heads_in[step][...].astype(F32)
    full = rows[...].reshape(size * tiles, width)
    for block in range(size):
        blocks[block] = full[:, block * mine : (block + 1) * mine]
    first[...] = blocks[me]
    normed = normalise(full, gain[...]).astype(F32)
    for block in range(size):
        blocks[block] = normed[:, block * mine : (block + 1) * mine]
    out[...] = contract(blocks[me].astype(BF16), weight[...], 1, 0).astype(BF16)


def grouped(shape, axis, span):
    return lax.broadcasted_iota(jnp.int32, shape, axis) // span


def own_head(shape, heads):
    row = lax.broadcasted_iota(jnp.int32, shape, 0) % heads
    return row == grouped(shape, 1, VHD)


def fold_kernel(size, heads, place, *refs):
    parts, weight, outs, folded = refs[:size], refs[size], refs[size + 1 : -1], refs[-1]
    me = place[0] % size
    total = parts[0][...].astype(F32)
    for step in range(1, size):
        total = total + parts[step][...].astype(F32)
    count, _ = total.shape
    spots = (count * heads, count)
    repeat = grouped(spots, 0, heads) == lax.broadcasted_iota(jnp.int32, spots, 1)
    repeated = contract(repeat.astype(F32).astype(BF16), total.astype(BF16), 1, 0)
    blocked = jnp.where(own_head(repeated.shape, heads), repeated, 0.0).astype(BF16)
    folded[...] = contract(blocked, weight[...], 1, 1).astype(BF16).reshape(folded.shape)
    for step in range(size):
        outs[step][...] = folded[other(me, step, size)]


def cut_kernel(size, place, weight, after, *refs):
    outs, blocks = refs[:-1], refs[-1]
    me = place[0] % size
    mine = weight.shape[1] // size
    for block in range(size):
        blocks[block] = weight[:, block * mine : (block + 1) * mine]
    for step in range(size):
        outs[step][...] = blocks[other(me, step, size)]


def token_kernel(size, heads, place, *refs):
    parts, normed, outs, (blocks, folded) = (
        refs[:size],
        refs[size],
        refs[size + 1 : -2],
        refs[-2:],
    )
    me = place[0] % size
    rows = parts[0].shape[1]
    for step in range(size):
        blocks[source(me, step, size)] = parts[step][...]
    for block in range(size):
        folded[:, block * rows : (block + 1) * rows] = blocks[block]
    tiles, patches, width = normed.shape
    tokens = normed[...].reshape(tiles * patches, width)
    scores = contract(folded[...], tokens, 1, 1) / math.sqrt(VHD)
    same = grouped(scores.shape, 0, heads) == grouped(scores.shape, 1, patches)
    lifted = jnp.where(same, jnp.exp(scores), 0.0)
    probs = (lifted / jnp.sum(lifted, axis=-1, keepdims=True)).astype(BF16)
    mixed = contract(probs, tokens, 1, 0).astype(BF16)
    for block in range(size):
        blocks[block] = mixed[:, block * rows : (block + 1) * rows]
    for step in range(size):
        outs[step][...] = blocks[other(me, step, size)]


def value_kernel(size, heads, place, *refs):
    parts, (weight, out, mixed) = refs[:size], refs[size:]
    me = place[0] % size
    for step in range(size):
        mixed[source(me, step, size)] = parts[step][...]
    rows = mixed[...].reshape(size * parts[0].shape[0], parts[0].shape[1])
    product = contract(rows, weight[...], 1, 0)
    kept = jnp.where(own_head(product.shape, heads), product, 0.0).astype(BF16)
    spots = (out.shape[0], product.shape[0])
    collect = lax.broadcasted_iota(jnp.int32, spots, 0) == grouped(spots, 1, heads)
    out[...] = contract(collect.astype(F32).astype(BF16), kept, 1, 0).astype(BF16)


def embed_kernel(size, place, *refs):
    parts, blocks, (first, project, notes, out, weight) = (
        refs[:size],
        refs[size : 2 * size],
        refs[2 * size :],
    )
    me = place[0] % size
    total = parts[0][...].astype(F32)
    for step in range(1, size):
        total = total + parts[step][...].astype(F32)
    pooled = total.astype(BF16)
    depth = blocks[0].shape[0]
    for step in range(size):
        start = pl.multiple_of(source(me, step, size) * depth, 16)
        weight[pl.ds(start, depth), :] = blocks[step][...]
    class_row = (first[...] + contract(pooled, weight[...], 1, 0)).astype(BF16)
    width = project.shape[1]
    out[:, :width] = contract(class_row, project[...], 1, 0).astype(BF16)
    out[:, width:] = notes[...]


def gather_kernel(*refs):
    parts, out = refs[1:-1], refs[-1]
    total = parts[0][...].astype(F32)
    for part in parts[1:]:
        total = total + part[...].astype(F32)
    width = total.shape[1] - LANES
    there = total[:, width + 2 : width + 3] > 0
    out[:, :width] = jnp.where(there, total[:, :width], 0.0).astype(BF16)
    out[:, width:] = total[:, width:].astype(BF16)


def along_lanes(column):
    shape = (column.shape[0], column.shape[0])
    here = lax.broadcasted_iota(jnp.int32, shape, 0) == lax.broadcasted_iota(jnp.int32, shape, 1)
    return jnp.sum(jnp.where(here, column, 0.0), axis=0, keepdims=True)


def slide_kernel(size, seq_size, place, *refs):
    parts = refs[:seq_size]
    gain, w_query, w_key, w_value = refs[seq_size : seq_size + 4]
    w_out, outs = refs[seq_size + 4 : seq_size + 4 + size], refs[seq_size + 4 + size :]
    me, seq = place[0] % size, place[0] // size
    rows = parts[0].shape[0]
    model = gain.shape[1]
    width = w_query.shape[0]
    total = rows * seq_size
    segment = total // 4
    tiles = jnp.concatenate([part[...].astype(F32) for part in parts], axis=0)
    notes = tiles[:, model:]
    position = along_lanes(notes[:, 0:1] * 256.0 + notes[:, 1:2]).astype(jnp.int32)
    here = along_lanes(notes[:, 2:3])
    normed = normalise(tiles[:, :model], gain[...])
    keys = contract(normed, w_key[...], 1, 1).astype(BF16)
    values = contract(normed, w_value[...], 1, 1).astype(BF16)
    asked = seq * rows + lax.broadcasted_iota(jnp.int32, (rows, total), 0)
    picker = jnp.where(asked == position, 1.0, 0.0).astype(BF16)
    mine = contract(picker, normed, 1, 0).astype(BF16)
    queries = contract(mine, w_query[...], 1, 1).astype(BF16).astype(F32)
    head_size = model // HEADS
    count = width // head_size
    shape = (count, rows, width)
    own = grouped(shape, 2, head_size) == lax.broadcasted_iota(jnp.int32, shape, 0)
    blocked = jnp.where(own, jnp.broadcast_to(queries[None], shape), 0.0)
    blocked = blocked.reshape(count * rows, width).astype(BF16)
    scores = contract(blocked, keys, 1, 1) / math.sqrt(head_size)
    line = lax.broadcasted_iota(jnp.int32, (count * rows, total), 0)
    asking = seq * rows + line % rows
    shift = (me * count + line // rows) % DILATION_STEP
    allowed = (here > 0) | (asking == position)
    near = (asking // segment == position // segment) & allowed
    far = (asking % DILATION_STEP == shift) & (position % DILATION_STEP == shift) & allowed
    times = jnp.where(near, 1.0, 0.0) + jnp.where(far, 1.0, 0.0)
    lifted = jnp.where(times > 0, jnp.exp(scores), 0.0)
    bottom = jnp.sum(lifted * times, axis=-1, keepdims=True)
    weights = (lifted.astype(BF16).astype(F32) * times).astype(BF16)
    mixed = (contract(weights, values, 1, 0) / bottom).reshape(shape)
    attended = jnp.sum(jnp.where(own, mixed, 0.0), axis=0).astype(BF16)
    for step in range(size):
        outs[step][...] = contract(attended, w_out[step][...], 1, 0).astype(BF16)


def residual_kernel(size, seq_size, place, *refs):
    parts, (after, out, blocks) = refs[:seq_size], refs[seq_size:]
    me, seq = place[0] % size, place[0] // size
    rows, width = out.shape
    total = rows * seq_size
    tiles = jnp.concatenate([part[...].astype(F32) for part in parts], axis=0)
    notes = tiles[:, size * width :]
    position = along_lanes(notes[:, 0:1] * 256.0 + notes[:, 1:2]).astype(jnp.int32)
    asked = seq * rows + lax.broadcasted_iota(jnp.int32, (rows, total), 0)
    picker = jnp.where(asked == position, 1.0, 0.0).astype(BF16)
    mine = contract(picker, tiles[:, : size * width].astype(BF16), 1, 0)
    for block in range(size):
        blocks[block] = mine[:, block * width : (block + 1) * width]
    out[...] = blocks[me]


def local(
    tile_patches,
    vit_gain,
    w_query,
    w_key,
    w_value,
    w_out,
    w_proj,
    long_gain,
    long_query,
    long_key,
    long_value,
    long_out,
    seq_order,
    counts,
):
    size = lax.axis_size("fsdp")
    seq_size = lax.axis_size("seq")
    me = lax.axis_index("fsdp")
    place = (lax.axis_index("seq") * size + me).astype(jnp.int32).reshape(1)
    tiles, _, width = tile_patches.shape
    vit_width = w_key.shape[1]
    heads = vit_width // VHD
    rows = w_key.shape[0]
    model = w_proj.shape[1]
    count = tiles * size

    head_row = pl.pallas_call(
        head_kernel,
        out_shape=jax.ShapeDtypeStruct((tiles, width), BF16),
        grid=(1,),
        in_specs=[pl.BlockSpec((tiles, 8, width), lambda i: (0, 0, 0))],
        out_specs=pl.BlockSpec(memory_space=pltpu.VMEM),
        compiler_params=pltpu.CompilerParams(vmem_limit_bytes=1 << 20),
        name="head",
    )(in_hbm(tile_patches))
    head_rows = spread(head_row, "fsdp")
    notes = call(
        functools.partial(notes_kernel, size),
        jax.ShapeDtypeStruct((count, LANES), BF16),
        [pltpu.VMEM((size, tiles, LANES), F32)],
        specs=[pltpu.SMEM, pltpu.SMEM, pl.ANY],
    )(place, seq_order, counts, head_row)

    def cut(weight, after):
        shape = (weight.shape[0], weight.shape[1] // size)
        return call(
            functools.partial(cut_kernel, size),
            [jax.ShapeDtypeStruct(shape, BF16)] * size,
            [pltpu.VMEM((size, *shape), BF16)],
            specs=[pl.ANY],
        )(place, weight, after)

    out_blocks = deal(cut(w_out, head_row), "fsdp")

    normed = normalise(tile_patches.astype(F32), vit_gain)

    gain_row = vit_gain[None, :]
    query_part, first = call(
        functools.partial(query_kernel, size),
        [
            jax.ShapeDtypeStruct((count, vit_width), BF16),
            jax.ShapeDtypeStruct((count, rows), F32),
        ],
        [pltpu.VMEM((size, tiles, width), F32), pltpu.VMEM((size, count, rows), F32)],
    )(place, *head_rows, gain_row, w_query)
    query_parts = spread(query_part, "fsdp")

    block = jax.ShapeDtypeStruct((tiles * heads, rows), BF16)
    folded = call(
        functools.partial(fold_kernel, size, heads),
        [block] * size,
        [pltpu.VMEM((size, tiles * heads, rows), BF16)],
    )(place, *query_parts, w_key)
    folded = deal(folded, "fsdp")

    mixed = call(
        functools.partial(token_kernel, size, heads),
        [block] * size,
        [pltpu.VMEM((size, tiles * heads, rows), BF16), pltpu.VMEM((tiles * heads, width), BF16)],
    )(place, *folded, normed)
    mixed = deal(mixed, "fsdp")

    pooled_part = call(
        functools.partial(value_kernel, size, heads),
        jax.ShapeDtypeStruct((count, vit_width), BF16),
        [pltpu.VMEM((size, tiles * heads, rows), BF16)],
    )(place, *mixed, w_value)
    pooled_parts = spread(pooled_part, "fsdp")

    embed_part = call(
        functools.partial(embed_kernel, size),
        jax.ShapeDtypeStruct((count, model + LANES), BF16),
        [pltpu.VMEM((vit_width, width // size), BF16)],
    )(place, *pooled_parts, *out_blocks, first, w_proj, notes)
    embed_parts = spread(embed_part, "fsdp")

    group_tiles = call(
        gather_kernel, jax.ShapeDtypeStruct((count, model + LANES), BF16)
    )(place, *embed_parts)
    all_tiles = rows_of_all(group_tiles)

    head_width = long_query.shape[1]
    long_blocks = cut(long_out, pooled_part)
    block = jax.ShapeDtypeStruct((count, head_width), BF16)
    terms = call(functools.partial(slide_kernel, size, seq_size), [block] * size)(
        place,
        *all_tiles,
        long_gain[None, :],
        jnp.transpose(long_query),
        jnp.transpose(long_key),
        jnp.transpose(long_value),
        *long_blocks,
    )
    residual = call(
        functools.partial(residual_kernel, size, seq_size),
        jax.ShapeDtypeStruct((count, head_width), F32),
        [pltpu.VMEM((size, count, head_width), F32)],
        specs=[pl.ANY],
    )(place, *all_tiles, terms[0])
    terms = deal(terms, "fsdp")
    summed = terms[0].astype(F32)
    for step in range(1, size):
        summed = summed + terms[step].astype(F32)
    return (residual + summed).astype(BF16)


def solution(mesh):
    return jax.shard_map(
        local,
        mesh=mesh,
        in_specs=(
            P(("group", "seq", "fsdp"), None, None),
            P(),
            P("fsdp", None),
            P("fsdp", None),
            P("fsdp", None),
            P("fsdp", None),
            P("fsdp", None),
            P(),
            P(None, "fsdp"),
            P(None, "fsdp"),
            P(None, "fsdp"),
            P("fsdp", None),
            P(("group", "seq", "fsdp")),
            P(("group", "seq", "fsdp")),
        ),
        out_specs=P(("group", "seq"), "fsdp"),
        check_vma=False,
    )
```

```python
import functools
import math

import jax
import jax.numpy as jnp
from jax import lax
from jax.experimental import pallas as pl
from jax.experimental.pallas import tpu as pltpu
from jax.sharding import PartitionSpec as P


VHD = 64
HEADS = 16
DILATION_STEP = 4
EPSILON = 1e-06
LANES = 128


BF16 = jnp.bfloat16
F32 = jnp.float32


def other(index, step, size):
    return index ^ step if size & (size - 1) == 0 else (index + step) % size


def source(index, step, size):
    return index ^ step if size & (size - 1) == 0 else (index + size - step) % size


def swap(array, axis, step):
    size = lax.axis_size(axis)
    return lax.ppermute(array, axis, [(i, other(i, step, size)) for i in range(size)])


def spread(array, axis):
    return [array] + [swap(array, axis, step) for step in range(1, lax.axis_size(axis))]


def rows_of_all(array):
    size, seq_size = lax.axis_size("fsdp"), lax.axis_size("seq")
    if size % 2 or seq_size & (seq_size - 1) or seq_size < 4:
        return spread(array, "seq")
    pairs = [
        (row * size + place, (row ^ (2 + place % 2)) * size + place)
        for row in range(seq_size)
        for place in range(size)
    ]
    far = lax.ppermute(array, ("seq", "fsdp"), pairs)
    steps = [1, *range(4, seq_size)]
    direct = [swap(array, "seq", step) for step in steps]
    return [array, far, swap(far, "fsdp", 1), *direct]


def deal(arrays, axis):
    return [arrays[0]] + [swap(arrays[step], axis, step) for step in range(1, len(arrays))]


def normalise(rows, gain):
    average = jnp.mean(rows, axis=-1, keepdims=True)
    centred = rows - average
    variance = jnp.mean(centred * centred, axis=-1, keepdims=True)
    return (centred * lax.rsqrt(variance + EPSILON) * gain).astype(BF16)


def contract(left, right, left_axis, right_axis):
    return lax.dot_general(
        left, right, (((left_axis,), (right_axis,)), ((), ())), preferred_element_type=F32
    )


def in_hbm(array):
    return pltpu.with_memory_space_constraint(array, pltpu.HBM)


def call(body, outs, scratch=(), limit=1 << 23, specs=()):
    smem, vmem = pl.BlockSpec(memory_space=pltpu.SMEM), pl.BlockSpec(memory_space=pltpu.VMEM)

    def run(place, *arrays):
        last = len(arrays) - len(specs)
        return pl.pallas_call(
            body,
            out_shape=outs,
            in_specs=[smem] + [vmem] * last + [pl.BlockSpec(memory_space=m) for m in specs],
            out_specs=jax.tree.map(lambda _: vmem, outs),
            scratch_shapes=list(scratch),
            compiler_params=pltpu.CompilerParams(vmem_limit_bytes=limit),
        )(place, *arrays)

    return run


def head_kernel(tokens, out):
    for tile in range(tokens.shape[0]):
        out[tile : tile + 1, :] = tokens[tile, 0:1, :]


def notes_kernel(size, place, order, counts, after, out, rows):
    me = place[0] % size
    tiles = order.shape[0]
    lane = lax.broadcasted_iota(jnp.int32, (1, LANES), 1)
    rows[...] = jnp.zeros_like(rows)
    for tile in range(tiles):
        spot = order[tile]
        present = (counts[0] > tile).astype(jnp.int32)
        high = jnp.where(lane == 0, spot // 256, 0)
        low = jnp.where(lane == 1, spot % 256, 0)
        notes = high + low + jnp.where(lane == 2, present, 0)
        rows[me, tile : tile + 1, :] = notes.astype(F32)
    out[...] = rows[...].reshape(size * tiles, LANES).astype(BF16)


def query_kernel(size, place, *refs):
    heads_in, (gain, weight, out, first, rows, blocks) = refs[:size], refs[size:]
    me = place[0] % size
    tiles, width = heads_in[0].shape
    mine = weight.shape[0]
    for step in range(size):
        rows[source(me, step, size)] = heads_in[step][...].astype(F32)
    full = rows[...].reshape(size * tiles, width)
    for block in range(size):
        blocks[block] = full[:, block * mine : (block + 1) * mine]
    first[...] = blocks[me]
    normed = normalise(full, gain[...]).astype(F32)
    for block in range(size):
        blocks[block] = normed[:, block * mine : (block + 1) * mine]
    out[...] = contract(blocks[me].astype(BF16), weight[...], 1, 0).astype(BF16)


def grouped(shape, axis, span):
    return lax.broadcasted_iota(jnp.int32, shape, axis) // span


def own_head(shape, heads):
    row = lax.broadcasted_iota(jnp.int32, shape, 0) % heads
    return row == grouped(shape, 1, VHD)


def fold_kernel(size, heads, place, *refs):
    parts, weight, outs, folded = refs[:size], refs[size], refs[size + 1 : -1], refs[-1]
    me = place[0] % size
    total = parts[0][...].astype(F32)
    for step in range(1, size):
        total = total + parts[step][...].astype(F32)
    count, _ = total.shape
    spots = (count * heads, count)
    repeat = grouped(spots, 0, heads) == lax.broadcasted_iota(jnp.int32, spots, 1)
    repeated = contract(repeat.astype(F32).astype(BF16), total.astype(BF16), 1, 0)
    blocked = jnp.where(own_head(repeated.shape, heads), repeated, 0.0).astype(BF16)
    folded[...] = contract(blocked, weight[...], 1, 1).astype(BF16).reshape(folded.shape)
    for step in range(size):
        outs[step][...] = folded[other(me, step, size)]


def cut_kernel(size, place, weight, after, *refs):
    outs, blocks = refs[:-1], refs[-1]
    me = place[0] % size
    mine = weight.shape[1] // size
    for block in range(size):
        blocks[block] = weight[:, block * mine : (block + 1) * mine]
    for step in range(size):
        outs[step][...] = blocks[other(me, step, size)]


def token_kernel(size, heads, place, *refs):
    parts, normed, outs, (blocks, folded) = (
        refs[:size],
        refs[size],
        refs[size + 1 : -2],
        refs[-2:],
    )
    me = place[0] % size
    rows = parts[0].shape[1]
    for step in range(size):
        blocks[source(me, step, size)] = parts[step][...]
    for block in range(size):
        folded[:, block * rows : (block + 1) * rows] = blocks[block]
    tiles, patches, width = normed.shape
    tokens = normed[...].reshape(tiles * patches, width)
    scores = contract(folded[...], tokens, 1, 1) / math.sqrt(VHD)
    same = grouped(scores.shape, 0, heads) == grouped(scores.shape, 1, patches)
    lifted = jnp.where(same, jnp.exp(scores), 0.0)
    probs = (lifted / jnp.sum(lifted, axis=-1, keepdims=True)).astype(BF16)
    mixed = contract(probs, tokens, 1, 0).astype(BF16)
    for block in range(size):
        blocks[block] = mixed[:, block * rows : (block + 1) * rows]
    for step in range(size):
        outs[step][...] = blocks[other(me, step, size)]


def value_kernel(size, heads, place, *refs):
    parts, (weight, out, mixed) = refs[:size], refs[size:]
    me = place[0] % size
    for step in range(size):
        mixed[source(me, step, size)] = parts[step][...]
    rows = mixed[...].reshape(size * parts[0].shape[0], parts[0].shape[1])
    product = contract(rows, weight[...], 1, 0)
    kept = jnp.where(own_head(product.shape, heads), product, 0.0).astype(BF16)
    spots = (out.shape[0], product.shape[0])
    collect = lax.broadcasted_iota(jnp.int32, spots, 0) == grouped(spots, 1, heads)
    out[...] = contract(collect.astype(F32).astype(BF16), kept, 1, 0).astype(BF16)


def embed_kernel(size, place, *refs):
    parts, blocks, (first, project, notes, out, weight) = (
        refs[:size],
        refs[size : 2 * size],
        refs[2 * size :],
    )
    me = place[0] % size
    total = parts[0][...].astype(F32)
    for step in range(1, size):
        total = total + parts[step][...].astype(F32)
    pooled = total.astype(BF16)
    depth = blocks[0].shape[0]
    for step in range(size):
        start = pl.multiple_of(source(me, step, size) * depth, 16)
        weight[pl.ds(start, depth), :] = blocks[step][...]
    class_row = (first[...] + contract(pooled, weight[...], 1, 0)).astype(BF16)
    width = project.shape[1]
    out[:, :width] = contract(class_row, project[...], 1, 0).astype(BF16)
    out[:, width:] = notes[...]


def gather_kernel(*refs):
    parts, out = refs[1:-1], refs[-1]
    total = parts[0][...].astype(F32)
    for part in parts[1:]:
        total = total + part[...].astype(F32)
    width = total.shape[1] - LANES
    there = total[:, width + 2 : width + 3] > 0
    out[:, :width] = jnp.where(there, total[:, :width], 0.0).astype(BF16)
    out[:, width:] = total[:, width:].astype(BF16)


def along_lanes(column):
    shape = (column.shape[0], column.shape[0])
    here = lax.broadcasted_iota(jnp.int32, shape, 0) == lax.broadcasted_iota(jnp.int32, shape, 1)
    return jnp.sum(jnp.where(here, column, 0.0), axis=0, keepdims=True)


def slide_kernel(size, seq_size, place, *refs):
    parts = refs[:seq_size]
    gain, w_query, w_key, w_value = refs[seq_size : seq_size + 4]
    w_out, outs = refs[seq_size + 4 : seq_size + 4 + size], refs[seq_size + 4 + size :]
    me, seq = place[0] % size, place[0] // size
    rows = parts[0].shape[0]
    model = gain.shape[1]
    width = w_query.shape[0]
    total = rows * seq_size
    segment = total // 4
    tiles = jnp.concatenate([part[...].astype(F32) for part in parts], axis=0)
    notes = tiles[:, model:]
    position = along_lanes(notes[:, 0:1] * 256.0 + notes[:, 1:2]).astype(jnp.int32)
    here = along_lanes(notes[:, 2:3])
    normed = normalise(tiles[:, :model], gain[...])
    keys = contract(normed, w_key[...], 1, 1).astype(BF16)
    values = contract(normed, w_value[...], 1, 1).astype(BF16)
    asked = seq * rows + lax.broadcasted_iota(jnp.int32, (rows, total), 0)
    picker = jnp.where(asked == position, 1.0, 0.0).astype(BF16)
    mine = contract(picker, normed, 1, 0).astype(BF16)
    queries = contract(mine, w_query[...], 1, 1).astype(BF16).astype(F32)
    head_size = model // HEADS
    count = width // head_size
    shape = (count, rows, width)
    own = grouped(shape, 2, head_size) == lax.broadcasted_iota(jnp.int32, shape, 0)
    blocked = jnp.where(own, jnp.broadcast_to(queries[None], shape), 0.0)
    blocked = blocked.reshape(count * rows, width).astype(BF16)
    scores = contract(blocked, keys, 1, 1) / math.sqrt(head_size)
    line = lax.broadcasted_iota(jnp.int32, (count * rows, total), 0)
    asking = seq * rows + line % rows
    shift = (me * count + line // rows) % DILATION_STEP
    allowed = (here > 0) | (asking == position)
    near = (asking // segment == position // segment) & allowed
    far = (asking % DILATION_STEP == shift) & (position % DILATION_STEP == shift) & allowed
    times = jnp.where(near, 1.0, 0.0) + jnp.where(far, 1.0, 0.0)
    lifted = jnp.where(times > 0, jnp.exp(scores), 0.0)
    bottom = jnp.sum(lifted * times, axis=-1, keepdims=True)
    weights = (lifted.astype(BF16).astype(F32) * times).astype(BF16)
    mixed = (contract(weights, values, 1, 0) / bottom).reshape(shape)
    attended = jnp.sum(jnp.where(own, mixed, 0.0), axis=0).astype(BF16)
    for step in range(size):
        outs[step][...] = contract(attended, w_out[step][...], 1, 0).astype(BF16)


def residual_kernel(size, seq_size, place, *refs):
    parts, (after, out, blocks) = refs[:seq_size], refs[seq_size:]
    me, seq = place[0] % size, place[0] // size
    rows, width = out.shape
    total = rows * seq_size
    tiles = jnp.concatenate([part[...].astype(F32) for part in parts], axis=0)
    notes = tiles[:, size * width :]
    position = along_lanes(notes[:, 0:1] * 256.0 + notes[:, 1:2]).astype(jnp.int32)
    asked = seq * rows + lax.broadcasted_iota(jnp.int32, (rows, total), 0)
    picker = jnp.where(asked == position, 1.0, 0.0).astype(BF16)
    mine = contract(picker, tiles[:, : size * width].astype(BF16), 1, 0)
    for block in range(size):
        blocks[block] = mine[:, block * width : (block + 1) * width]
    out[...] = blocks[me]


def local(
    tile_patches,
    vit_gain,
    w_query,
    w_key,
    w_value,
    w_out,
    w_proj,
    long_gain,
    long_query,
    long_key,
    long_value,
    long_out,
    seq_order,
    counts,
):
    size = lax.axis_size("fsdp")
    seq_size = lax.axis_size("seq")
    me = lax.axis_index("fsdp")
    place = (lax.axis_index("seq") * size + me).astype(jnp.int32).reshape(1)
    tiles, _, width = tile_patches.shape
    vit_width = w_key.shape[1]
    heads = vit_width // VHD
    rows = w_key.shape[0]
    model = w_proj.shape[1]
    count = tiles * size

    head_row = pl.pallas_call(
        head_kernel,
        out_shape=jax.ShapeDtypeStruct((tiles, width), BF16),
        grid=(1,),
        in_specs=[pl.BlockSpec((tiles, 8, width), lambda i: (0, 0, 0))],
        out_specs=pl.BlockSpec(memory_space=pltpu.VMEM),
        compiler_params=pltpu.CompilerParams(vmem_limit_bytes=1 << 20),
        name="head",
    )(in_hbm(tile_patches))
    head_rows = spread(head_row, "fsdp")
    notes = call(
        functools.partial(notes_kernel, size),
        jax.ShapeDtypeStruct((count, LANES), BF16),
        [pltpu.VMEM((size, tiles, LANES), F32)],
        specs=[pltpu.SMEM, pltpu.SMEM, pl.ANY],
    )(place, seq_order, counts, head_row)

    def cut(weight, after):
        shape = (weight.shape[0], weight.shape[1] // size)
        return call(
            functools.partial(cut_kernel, size),
            [jax.ShapeDtypeStruct(shape, BF16)] * size,
            [pltpu.VMEM((size, *shape), BF16)],
            specs=[pl.ANY],
        )(place, weight, after)

    out_blocks = deal(cut(w_out, head_row), "fsdp")

    normed = normalise(tile_patches.astype(F32), vit_gain)

    gain_row = vit_gain[None, :]
    query_part, first = call(
        functools.partial(query_kernel, size),
        [
            jax.ShapeDtypeStruct((count, vit_width), BF16),
            jax.ShapeDtypeStruct((count, rows), F32),
        ],
        [pltpu.VMEM((size, tiles, width), F32), pltpu.VMEM((size, count, rows), F32)],
    )(place, *head_rows, gain_row, w_query)
    query_parts = spread(query_part, "fsdp")

    block = jax.ShapeDtypeStruct((tiles * heads, rows), BF16)
    folded = call(
        functools.partial(fold_kernel, size, heads),
        [block] * size,
        [pltpu.VMEM((size, tiles * heads, rows), BF16)],
    )(place, *query_parts, w_key)
    folded = deal(folded, "fsdp")

    mixed = call(
        functools.partial(token_kernel, size, heads),
        [block] * size,
        [pltpu.VMEM((size, tiles * heads, rows), BF16), pltpu.VMEM((tiles * heads, width), BF16)],
    )(place, *folded, normed)
    mixed = deal(mixed, "fsdp")

    pooled_part = call(
        functools.partial(value_kernel, size, heads),
        jax.ShapeDtypeStruct((count, vit_width), BF16),
        [pltpu.VMEM((size, tiles * heads, rows), BF16)],
    )(place, *mixed, w_value)
    pooled_parts = spread(pooled_part, "fsdp")

    embed_part = call(
        functools.partial(embed_kernel, size),
        jax.ShapeDtypeStruct((count, model + LANES), BF16),
        [pltpu.VMEM((vit_width, width // size), BF16)],
    )(place, *pooled_parts, *out_blocks, first, w_proj, notes)
    embed_parts = spread(embed_part, "fsdp")

    group_tiles = call(
        gather_kernel, jax.ShapeDtypeStruct((count, model + LANES), BF16)
    )(place, *embed_parts)
    all_tiles = rows_of_all(group_tiles)

    head_width = long_query.shape[1]
    long_blocks = cut(long_out, pooled_part)
    block = jax.ShapeDtypeStruct((count, head_width), BF16)
    terms = call(functools.partial(slide_kernel, size, seq_size), [block] * size)(
        place,
        *all_tiles,
        long_gain[None, :],
        jnp.transpose(long_query),
        jnp.transpose(long_key),
        jnp.transpose(long_value),
        *long_blocks,
    )
    residual = call(
        functools.partial(residual_kernel, size, seq_size),
        jax.ShapeDtypeStruct((count, head_width), F32),
        [pltpu.VMEM((size, count, head_width), F32)],
        specs=[pl.ANY],
    )(place, *all_tiles, terms[0])
    terms = deal(terms, "fsdp")
    summed = terms[0].astype(F32)
    for step in range(1, size):
        summed = summed + terms[step].astype(F32)
    return (residual + summed).astype(BF16)


def solution(mesh):
    return jax.shard_map(
        local,
        mesh=mesh,
        in_specs=(
            P(("group", "seq", "fsdp"), None, None),
            P(),
            P("fsdp", None),
            P("fsdp", None),
            P("fsdp", None),
            P("fsdp", None),
            P("fsdp", None),
            P(),
            P(None, "fsdp"),
            P(None, "fsdp"),
            P(None, "fsdp"),
            P("fsdp", None),
            P(("group", "seq", "fsdp")),
            P(("group", "seq", "fsdp")),
        ),
        out_specs=P(("group", "seq"), "fsdp"),
        check_vma=False,
    )
```

```python
import functools
import math

import jax
import jax.numpy as jnp
from jax import lax
from jax.experimental import pallas as pl
from jax.experimental.pallas import tpu as pltpu
from jax.sharding import PartitionSpec as P


VHD = 64
HEADS = 16
DILATION_STEP = 4
EPSILON = 1e-06
LANES = 128


BF16 = jnp.bfloat16
F32 = jnp.float32


def other(index, step, size):
    return index ^ step if size & (size - 1) == 0 else (index + step) % size


def source(index, step, size):
    return index ^ step if size & (size - 1) == 0 else (index + size - step) % size


def swap(array, axis, step):
    size = lax.axis_size(axis)
    return lax.ppermute(array, axis, [(i, other(i, step, size)) for i in range(size)])


def spread(array, axis):
    return [array] + [swap(array, axis, step) for step in range(1, lax.axis_size(axis))]


def rows_of_all(array):
    size, seq_size = lax.axis_size("fsdp"), lax.axis_size("seq")
    if size % 2 or seq_size & (seq_size - 1) or seq_size < 4:
        return spread(array, "seq")
    pairs = [
        (row * size + place, (row ^ (2 + place % 2)) * size + place)
        for row in range(seq_size)
        for place in range(size)
    ]
    far = lax.ppermute(array, ("seq", "fsdp"), pairs)
    steps = [1, *range(4, seq_size)]
    direct = [swap(array, "seq", step) for step in steps]
    return [array, far, swap(far, "fsdp", 1), *direct]


def deal(arrays, axis):
    return [arrays[0]] + [swap(arrays[step], axis, step) for step in range(1, len(arrays))]


def normalise(rows, gain):
    average = jnp.mean(rows, axis=-1, keepdims=True)
    centred = rows - average
    variance = jnp.mean(centred * centred, axis=-1, keepdims=True)
    return (centred * lax.rsqrt(variance + EPSILON) * gain).astype(BF16)


def contract(left, right, left_axis, right_axis):
    return lax.dot_general(
        left, right, (((left_axis,), (right_axis,)), ((), ())), preferred_element_type=F32
    )


def in_hbm(array):
    return pltpu.with_memory_space_constraint(array, pltpu.HBM)


def call(body, outs, scratch=(), limit=1 << 23, specs=()):
    smem, vmem = pl.BlockSpec(memory_space=pltpu.SMEM), pl.BlockSpec(memory_space=pltpu.VMEM)

    def run(place, *arrays):
        last = len(arrays) - len(specs)
        return pl.pallas_call(
            body,
            out_shape=outs,
            in_specs=[smem] + [vmem] * last + [pl.BlockSpec(memory_space=m) for m in specs],
            out_specs=jax.tree.map(lambda _: vmem, outs),
            scratch_shapes=list(scratch),
            compiler_params=pltpu.CompilerParams(vmem_limit_bytes=limit),
        )(place, *arrays)

    return run


def head_kernel(tokens, out):
    for tile in range(tokens.shape[0]):
        out[tile : tile + 1, :] = tokens[tile, 0:1, :]


def notes_kernel(size, place, order, counts, after, out, rows):
    me = place[0] % size
    tiles = order.shape[0]
    lane = lax.broadcasted_iota(jnp.int32, (1, LANES), 1)
    rows[...] = jnp.zeros_like(rows)
    for tile in range(tiles):
        spot = order[tile]
        present = (counts[0] > tile).astype(jnp.int32)
        high = jnp.where(lane == 0, spot // 256, 0)
        low = jnp.where(lane == 1, spot % 256, 0)
        notes = high + low + jnp.where(lane == 2, present, 0)
        rows[me, tile : tile + 1, :] = notes.astype(F32)
    out[...] = rows[...].reshape(size * tiles, LANES).astype(BF16)


def halve_kernel(place, weight, after, kept, sent, halves):
    mine = place[0] % 2
    half = kept.shape[1]
    for block in range(2):
        halves[block] = weight[:, block * half : (block + 1) * half]
    kept[...] = halves[mine]
    sent[...] = halves[1 - mine]


def query_kernel(size, place, *refs):
    heads_in, (gain, kept, fetched, out, first, rows, blocks) = refs[:size], refs[size:]
    me = place[0] % size
    tiles, width = heads_in[0].shape
    mine = kept.shape[0]
    for step in range(size):
        rows[source(me, step, size)] = heads_in[step][...].astype(F32)
    full = rows[...].reshape(size * tiles, width)
    for block in range(size):
        blocks[block] = full[:, block * mine : (block + 1) * mine]
    first[...] = blocks[me]
    normed = normalise(full, gain[...]).astype(F32)
    for block in range(size):
        blocks[block] = normed[:, block * mine : (block + 1) * mine]
    part = contract(blocks[me].astype(BF16), kept[...], 1, 0)
    part = part + contract(blocks[me ^ 1].astype(BF16), fetched[...], 1, 0)
    out[...] = part.astype(BF16)


def grouped(shape, axis, span):
    return lax.broadcasted_iota(jnp.int32, shape, axis) // span


def own_head(shape, tiles, half):
    row = lax.broadcasted_iota(jnp.int32, shape, 0)
    return row // (tiles * half) % 2 * half + row % half == grouped(shape, 1, VHD)


def own_tile(row, tiles, half):
    return row // (2 * tiles * half) * tiles + row % (tiles * half) // half


def fold_kernel(size, half, place, *refs):
    parts, (kept, fetched) = refs[: size // 2], refs[size // 2 : size // 2 + 2]
    outs, folded = refs[size // 2 + 2 : -1], refs[-1]
    me = place[0] % size
    total = parts[0][...].astype(F32)
    for part in parts[1:]:
        total = total + part[...].astype(F32)
    count, _ = total.shape
    spots = (count * half, count)
    repeat = grouped(spots, 0, half) == lax.broadcasted_iota(jnp.int32, spots, 1)
    repeated = contract(repeat.astype(F32).astype(BF16), total.astype(BF16), 1, 0)
    shape = repeated.shape
    own = lax.broadcasted_iota(jnp.int32, shape, 0) % half == grouped(shape, 1, VHD)
    blocked = jnp.where(own, repeated, 0.0).astype(BF16)
    for at, weight in ((me % 2, kept), (1 - me % 2, fetched)):
        product = contract(blocked, weight[...], 1, 1)
        product = product.reshape(size, product.shape[0] // size, product.shape[1])
        for owner in range(size):
            folded[owner, at] = product[owner]
    for step in range(size):
        piece = folded[other(me, step, size)]
        outs[step][...] = piece.reshape(outs[step].shape).astype(BF16)


def cut_kernel(size, place, weight, after, *refs):
    outs, blocks = refs[:-1], refs[-1]
    me = place[0] % size
    mine = weight.shape[1] // size
    for block in range(size):
        blocks[block] = weight[:, block * mine : (block + 1) * mine]
    for step in range(size):
        outs[step][...] = blocks[other(me, step, size)]


def token_kernel(size, half, place, *refs):
    parts, normed, outs, (pieces, blocks, folded) = (
        refs[:size],
        refs[size],
        refs[size + 1 : -3],
        refs[-3:],
    )
    me = place[0] % size
    rows = parts[0].shape[1]
    tiles, patches, width = normed.shape
    for step in range(size):
        sender = source(me, step, size)
        at = sender % 2
        part = parts[step][...].astype(F32).reshape(2, tiles * half, rows)
        for block in range(2):
            pieces[sender - at + block, at] = part[block]
    for block in range(size):
        piece = pieces[block].reshape(folded.shape[0], rows).astype(BF16)
        folded[:, block * rows : (block + 1) * rows] = piece
    tokens = normed[...].reshape(tiles * patches, width)
    scores = contract(folded[...], tokens, 1, 1) / math.sqrt(VHD)
    row = lax.broadcasted_iota(jnp.int32, scores.shape, 0)
    same = own_tile(row, tiles, half) == grouped(scores.shape, 1, patches)
    lifted = jnp.where(same, jnp.exp(scores), 0.0)
    probs = (lifted / jnp.sum(lifted, axis=-1, keepdims=True)).astype(BF16)
    mixed = contract(probs, tokens, 1, 0).astype(BF16)
    for block in range(size):
        blocks[block] = mixed[:, block * rows : (block + 1) * rows]
    for step in range(size):
        outs[step][...] = blocks[other(me, step, size)]


def value_kernel(size, tiles, half, place, *refs):
    parts, (weight, out, mixed) = refs[:size], refs[size:]
    me = place[0] % size
    for step in range(size):
        mixed[source(me, step, size)] = parts[step][...]
    rows = mixed[...].reshape(size * parts[0].shape[0], parts[0].shape[1])
    product = contract(rows, weight[...], 1, 0)
    kept = jnp.where(own_head(product.shape, tiles, half), product, 0.0).astype(BF16)
    spots = (out.shape[0], product.shape[0])
    row = lax.broadcasted_iota(jnp.int32, spots, 1)
    collect = lax.broadcasted_iota(jnp.int32, spots, 0) == own_tile(row, tiles, half)
    out[...] = contract(collect.astype(F32).astype(BF16), kept, 1, 0).astype(BF16)


def embed_kernel(size, place, *refs):
    parts, blocks, (first, project, notes, out, weight) = (
        refs[:size],
        refs[size : 2 * size],
        refs[2 * size :],
    )
    me = place[0] % size
    total = parts[0][...].astype(F32)
    for step in range(1, size):
        total = total + parts[step][...].astype(F32)
    pooled = total.astype(BF16)
    depth = blocks[0].shape[0]
    for step in range(size):
        start = pl.multiple_of(source(me, step, size) * depth, 16)
        weight[pl.ds(start, depth), :] = blocks[step][...]
    class_row = (first[...] + contract(pooled, weight[...], 1, 0)).astype(BF16)
    width = project.shape[1]
    out[:, :width] = contract(class_row, project[...], 1, 0).astype(BF16)
    out[:, width:] = notes[...]


def gather_kernel(*refs):
    parts, out = refs[1:-1], refs[-1]
    total = parts[0][...].astype(F32)
    for part in parts[1:]:
        total = total + part[...].astype(F32)
    width = total.shape[1] - LANES
    there = total[:, width + 2 : width + 3] > 0
    out[:, :width] = jnp.where(there, total[:, :width], 0.0).astype(BF16)
    out[:, width:] = total[:, width:].astype(BF16)


def along_lanes(column):
    shape = (column.shape[0], column.shape[0])
    here = lax.broadcasted_iota(jnp.int32, shape, 0) == lax.broadcasted_iota(jnp.int32, shape, 1)
    return jnp.sum(jnp.where(here, column, 0.0), axis=0, keepdims=True)


def slide_kernel(size, seq_size, place, *refs):
    parts = refs[:seq_size]
    gain, w_query, w_key, w_value = refs[seq_size : seq_size + 4]
    w_out, outs = refs[seq_size + 4 : seq_size + 4 + size], refs[seq_size + 4 + size :]
    me, seq = place[0] % size, place[0] // size
    rows = parts[0].shape[0]
    model = gain.shape[1]
    width = w_query.shape[0]
    total = rows * seq_size
    segment = total // 4
    tiles = jnp.concatenate([part[...].astype(F32) for part in parts], axis=0)
    notes = tiles[:, model:]
    position = along_lanes(notes[:, 0:1] * 256.0 + notes[:, 1:2]).astype(jnp.int32)
    here = along_lanes(notes[:, 2:3])
    normed = normalise(tiles[:, :model], gain[...])
    keys = contract(normed, w_key[...], 1, 1).astype(BF16)
    values = contract(normed, w_value[...], 1, 1).astype(BF16)
    asked = seq * rows + lax.broadcasted_iota(jnp.int32, (rows, total), 0)
    picker = jnp.where(asked == position, 1.0, 0.0).astype(BF16)
    mine = contract(picker, normed, 1, 0).astype(BF16)
    queries = contract(mine, w_query[...], 1, 1).astype(BF16).astype(F32)
    head_size = model // HEADS
    count = width // head_size
    shape = (count, rows, width)
    own = grouped(shape, 2, head_size) == lax.broadcasted_iota(jnp.int32, shape, 0)
    blocked = jnp.where(own, jnp.broadcast_to(queries[None], shape), 0.0)
    blocked = blocked.reshape(count * rows, width).astype(BF16)
    scores = contract(blocked, keys, 1, 1) / math.sqrt(head_size)
    line = lax.broadcasted_iota(jnp.int32, (count * rows, total), 0)
    asking = seq * rows + line % rows
    shift = (me * count + line // rows) % DILATION_STEP
    allowed = (here > 0) | (asking == position)
    near = (asking // segment == position // segment) & allowed
    far = (asking % DILATION_STEP == shift) & (position % DILATION_STEP == shift) & allowed
    times = jnp.where(near, 1.0, 0.0) + jnp.where(far, 1.0, 0.0)
    lifted = jnp.where(times > 0, jnp.exp(scores), 0.0)
    bottom = jnp.sum(lifted * times, axis=-1, keepdims=True)
    weights = (lifted.astype(BF16).astype(F32) * times).astype(BF16)
    mixed = (contract(weights, values, 1, 0) / bottom).reshape(shape)
    attended = jnp.sum(jnp.where(own, mixed, 0.0), axis=0).astype(BF16)
    for step in range(size):
        outs[step][...] = contract(attended, w_out[step][...], 1, 0).astype(BF16)


def residual_kernel(size, seq_size, place, *refs):
    parts, (after, out, blocks) = refs[:seq_size], refs[seq_size:]
    me, seq = place[0] % size, place[0] // size
    rows, width = out.shape
    total = rows * seq_size
    tiles = jnp.concatenate([part[...].astype(F32) for part in parts], axis=0)
    notes = tiles[:, size * width :]
    position = along_lanes(notes[:, 0:1] * 256.0 + notes[:, 1:2]).astype(jnp.int32)
    asked = seq * rows + lax.broadcasted_iota(jnp.int32, (rows, total), 0)
    picker = jnp.where(asked == position, 1.0, 0.0).astype(BF16)
    mine = contract(picker, tiles[:, : size * width].astype(BF16), 1, 0)
    for block in range(size):
        blocks[block] = mine[:, block * width : (block + 1) * width]
    out[...] = blocks[me]


def local(
    tile_patches,
    vit_gain,
    w_query,
    w_key,
    w_value,
    w_out,
    w_proj,
    long_gain,
    long_query,
    long_key,
    long_value,
    long_out,
    seq_order,
    counts,
):
    size = lax.axis_size("fsdp")
    seq_size = lax.axis_size("seq")
    me = lax.axis_index("fsdp")
    place = (lax.axis_index("seq") * size + me).astype(jnp.int32).reshape(1)
    tiles, _, width = tile_patches.shape
    vit_width = w_key.shape[1]
    heads = vit_width // VHD
    rows = w_key.shape[0]
    model = w_proj.shape[1]
    count = tiles * size

    head_row = pl.pallas_call(
        head_kernel,
        out_shape=jax.ShapeDtypeStruct((tiles, width), BF16),
        grid=(1,),
        in_specs=[pl.BlockSpec((tiles, 8, width), lambda i: (0, 0, 0))],
        out_specs=pl.BlockSpec(memory_space=pltpu.VMEM),
        compiler_params=pltpu.CompilerParams(vmem_limit_bytes=1 << 20),
        name="head",
    )(in_hbm(tile_patches))
    head_rows = spread(head_row, "fsdp")
    notes = call(
        functools.partial(notes_kernel, size),
        jax.ShapeDtypeStruct((count, LANES), BF16),
        [pltpu.VMEM((size, tiles, LANES), F32)],
        specs=[pltpu.SMEM, pltpu.SMEM, pl.ANY],
    )(place, seq_order, counts, head_row)

    def cut(weight, after):
        shape = (weight.shape[0], weight.shape[1] // size)
        return call(
            functools.partial(cut_kernel, size),
            [jax.ShapeDtypeStruct(shape, BF16)] * size,
            [pltpu.VMEM((size, *shape), BF16)],
            specs=[pl.ANY],
        )(place, weight, after)

    out_blocks = deal(cut(w_out, head_row), "fsdp")

    normed = normalise(tile_patches.astype(F32), vit_gain)

    gain_row = vit_gain[None, :]

    def halve(weight, after):
        shape = jax.ShapeDtypeStruct((rows, vit_width // 2), BF16)
        kept, sent = call(
            halve_kernel,
            [shape, shape],
            [pltpu.VMEM((2, rows, vit_width // 2), BF16)],
            specs=[pl.ANY],
        )(place, weight, after)
        return kept, swap(sent, "fsdp", 1)

    query_part, first = call(
        functools.partial(query_kernel, size),
        [
            jax.ShapeDtypeStruct((count, vit_width // 2), BF16),
            jax.ShapeDtypeStruct((count, rows), F32),
        ],
        [pltpu.VMEM((size, tiles, width), F32), pltpu.VMEM((size, count, rows), F32)],
    )(place, *head_rows, gain_row, *halve(w_query, head_row))
    query_parts = [query_part]
    query_parts += [swap(query_part, "fsdp", step) for step in range(2, size, 2)]

    half = heads // 2
    block = jax.ShapeDtypeStruct((tiles * heads, rows), BF16)
    folded = call(
        functools.partial(fold_kernel, size, half),
        [block] * size,
        [pltpu.VMEM((size, 2, tiles * half, rows), F32)],
    )(place, *query_parts, *halve(w_key, query_part))
    folded = deal(folded, "fsdp")

    mixed = call(
        functools.partial(token_kernel, size, half),
        [block] * size,
        [
            pltpu.VMEM((size, 2, tiles * half, rows), F32),
            pltpu.VMEM((size, tiles * heads, rows), BF16),
            pltpu.VMEM((tiles * heads, width), BF16),
        ],
    )(place, *folded, normed)
    mixed = deal(mixed, "fsdp")

    pooled_part = call(
        functools.partial(value_kernel, size, tiles, half),
        jax.ShapeDtypeStruct((count, vit_width), BF16),
        [pltpu.VMEM((size, tiles * heads, rows), BF16)],
    )(place, *mixed, w_value)
    pooled_parts = spread(pooled_part, "fsdp")

    embed_part = call(
        functools.partial(embed_kernel, size),
        jax.ShapeDtypeStruct((count, model + LANES), BF16),
        [pltpu.VMEM((vit_width, width // size), BF16)],
    )(place, *pooled_parts, *out_blocks, first, w_proj, notes)
    embed_parts = spread(embed_part, "fsdp")

    group_tiles = call(
        gather_kernel, jax.ShapeDtypeStruct((count, model + LANES), BF16)
    )(place, *embed_parts)
    all_tiles = rows_of_all(group_tiles)

    head_width = long_query.shape[1]
    long_blocks = cut(long_out, pooled_part)
    block = jax.ShapeDtypeStruct((count, head_width), BF16)
    terms = call(functools.partial(slide_kernel, size, seq_size), [block] * size)(
        place,
        *all_tiles,
        long_gain[None, :],
        jnp.transpose(long_query),
        jnp.transpose(long_key),
        jnp.transpose(long_value),
        *long_blocks,
    )
    residual = call(
        functools.partial(residual_kernel, size, seq_size),
        jax.ShapeDtypeStruct((count, head_width), F32),
        [pltpu.VMEM((size, count, head_width), F32)],
        specs=[pl.ANY],
    )(place, *all_tiles, terms[0])
    terms = deal(terms, "fsdp")
    summed = terms[0].astype(F32)
    for step in range(1, size):
        summed = summed + terms[step].astype(F32)
    return (residual + summed).astype(BF16)


def solution(mesh):
    return jax.shard_map(
        local,
        mesh=mesh,
        in_specs=(
            P(("group", "seq", "fsdp"), None, None),
            P(),
            P("fsdp", None),
            P("fsdp", None),
            P("fsdp", None),
            P("fsdp", None),
            P("fsdp", None),
            P(),
            P(None, "fsdp"),
            P(None, "fsdp"),
            P(None, "fsdp"),
            P("fsdp", None),
            P(("group", "seq", "fsdp")),
            P(("group", "seq", "fsdp")),
        ),
        out_specs=P(("group", "seq"), "fsdp"),
        check_vma=False,
    )
```

```python
import functools
import math

import jax
import jax.numpy as jnp
from jax import lax
from jax.experimental import pallas as pl
from jax.experimental.pallas import tpu as pltpu
from jax.sharding import PartitionSpec as P


VHD = 64
HEADS = 16
DILATION_STEP = 4
EPSILON = 1e-06
LANES = 128


BF16 = jnp.bfloat16
F32 = jnp.float32


def other(index, step, size):
    return index ^ step if size & (size - 1) == 0 else (index + step) % size


def source(index, step, size):
    return index ^ step if size & (size - 1) == 0 else (index + size - step) % size


def swap(array, axis, step):
    size = lax.axis_size(axis)
    return lax.ppermute(array, axis, [(i, other(i, step, size)) for i in range(size)])


def spread(array, axis):
    return [array] + [swap(array, axis, step) for step in range(1, lax.axis_size(axis))]


def rows_of_all(array):
    size, seq_size = lax.axis_size("fsdp"), lax.axis_size("seq")
    if size % 2 or seq_size & (seq_size - 1) or seq_size < 4:
        return spread(array, "seq")
    pairs = [
        (row * size + place, (row ^ (2 + place % 2)) * size + place)
        for row in range(seq_size)
        for place in range(size)
    ]
    far = lax.ppermute(array, ("seq", "fsdp"), pairs)
    steps = [1, *range(4, seq_size)]
    direct = [swap(array, "seq", step) for step in steps]
    return [array, far, swap(far, "fsdp", 1), *direct]


def deal(arrays, axis):
    return [arrays[0]] + [swap(arrays[step], axis, step) for step in range(1, len(arrays))]


def normalise(rows, gain):
    average = jnp.mean(rows, axis=-1, keepdims=True)
    centred = rows - average
    variance = jnp.mean(centred * centred, axis=-1, keepdims=True)
    return (centred * lax.rsqrt(variance + EPSILON) * gain).astype(BF16)


def contract(left, right, left_axis, right_axis):
    return lax.dot_general(
        left, right, (((left_axis,), (right_axis,)), ((), ())), preferred_element_type=F32
    )


def in_hbm(array):
    return pltpu.with_memory_space_constraint(array, pltpu.HBM)


def call(body, outs, scratch=(), limit=1 << 23, specs=()):
    smem, vmem = pl.BlockSpec(memory_space=pltpu.SMEM), pl.BlockSpec(memory_space=pltpu.VMEM)

    def run(place, *arrays):
        last = len(arrays) - len(specs)
        return pl.pallas_call(
            body,
            out_shape=outs,
            in_specs=[smem] + [vmem] * last + [pl.BlockSpec(memory_space=m) for m in specs],
            out_specs=jax.tree.map(lambda _: vmem, outs),
            scratch_shapes=list(scratch),
            compiler_params=pltpu.CompilerParams(vmem_limit_bytes=limit),
        )(place, *arrays)

    return run


def head_kernel(tokens, out):
    for tile in range(tokens.shape[0]):
        out[tile : tile + 1, :] = tokens[tile, 0:1, :]


def notes_kernel(size, place, order, counts, after, out, rows):
    me = place[0] % size
    tiles = order.shape[0]
    lane = lax.broadcasted_iota(jnp.int32, (1, LANES), 1)
    rows[...] = jnp.zeros_like(rows)
    for tile in range(tiles):
        spot = order[tile]
        present = (counts[0] > tile).astype(jnp.int32)
        high = jnp.where(lane == 0, spot // 256, 0)
        low = jnp.where(lane == 1, spot % 256, 0)
        notes = high + low + jnp.where(lane == 2, present, 0)
        rows[me, tile : tile + 1, :] = notes.astype(F32)
    out[...] = rows[...].reshape(size * tiles, LANES).astype(BF16)


def halve_kernel(place, weight, after, kept, sent, halves):
    mine = place[0] % 2
    half = kept.shape[1]
    for block in range(2):
        halves[block] = weight[:, block * half : (block + 1) * half]
    kept[...] = halves[mine]
    sent[...] = halves[1 - mine]


def query_kernel(size, place, *refs):
    heads_in, (gain, kept, fetched, out, first, rows, blocks) = refs[:size], refs[size:]
    me = place[0] % size
    tiles, width = heads_in[0].shape
    mine = kept.shape[0]
    for step in range(size):
        rows[source(me, step, size)] = heads_in[step][...].astype(F32)
    full = rows[...].reshape(size * tiles, width)
    for block in range(size):
        blocks[block] = full[:, block * mine : (block + 1) * mine]
    first[...] = blocks[me]
    normed = normalise(full, gain[...]).astype(F32)
    for block in range(size):
        blocks[block] = normed[:, block * mine : (block + 1) * mine]
    part = contract(blocks[me].astype(BF16), kept[...], 1, 0)
    part = part + contract(blocks[me ^ 1].astype(BF16), fetched[...], 1, 0)
    out[...] = part


def grouped(shape, axis, span):
    return lax.broadcasted_iota(jnp.int32, shape, axis) // span


def own_head(shape, tiles, half):
    row = lax.broadcasted_iota(jnp.int32, shape, 0)
    return row // (tiles * half) % 2 * half + row % half == grouped(shape, 1, VHD)


def own_tile(row, tiles, half):
    return row // (2 * tiles * half) * tiles + row % (tiles * half) // half


def fold_kernel(size, half, place, *refs):
    parts, (kept, fetched) = refs[: size // 2], refs[size // 2 : size // 2 + 2]
    outs, folded = refs[size // 2 + 2 : -1], refs[-1]
    me = place[0] % size
    total = parts[0][...].astype(F32)
    for part in parts[1:]:
        total = total + part[...].astype(F32)
    count, _ = total.shape
    spots = (count * half, count)
    repeat = grouped(spots, 0, half) == lax.broadcasted_iota(jnp.int32, spots, 1)
    repeated = contract(repeat.astype(F32).astype(BF16), total.astype(BF16), 1, 0)
    shape = repeated.shape
    own = lax.broadcasted_iota(jnp.int32, shape, 0) % half == grouped(shape, 1, VHD)
    blocked = jnp.where(own, repeated, 0.0).astype(BF16)
    for at, weight in ((me % 2, kept), (1 - me % 2, fetched)):
        product = contract(blocked, weight[...], 1, 1)
        product = product.reshape(size, product.shape[0] // size, product.shape[1])
        for owner in range(size):
            folded[owner, at] = product[owner]
    for step in range(size):
        piece = folded[other(me, step, size)]
        outs[step][...] = piece.reshape(outs[step].shape).astype(BF16)


def cut_kernel(size, place, weight, after, *refs):
    outs, blocks = refs[:-1], refs[-1]
    me = place[0] % size
    mine = weight.shape[1] // size
    for block in range(size):
        blocks[block] = weight[:, block * mine : (block + 1) * mine]
    for step in range(size):
        outs[step][...] = blocks[other(me, step, size)]


def token_kernel(size, half, place, *refs):
    parts, normed, outs, (pieces, blocks, folded) = (
        refs[:size],
        refs[size],
        refs[size + 1 : -3],
        refs[-3:],
    )
    me = place[0] % size
    rows = parts[0].shape[1]
    tiles, patches, width = normed.shape
    for step in range(size):
        sender = source(me, step, size)
        at = sender % 2
        part = parts[step][...].astype(F32).reshape(2, tiles * half, rows)
        for block in range(2):
            pieces[sender - at + block, at] = part[block]
    for block in range(size):
        piece = pieces[block].reshape(folded.shape[0], rows).astype(BF16)
        folded[:, block * rows : (block + 1) * rows] = piece
    tokens = normed[...].reshape(tiles * patches, width)
    scores = contract(folded[...], tokens, 1, 1) / math.sqrt(VHD)
    row = lax.broadcasted_iota(jnp.int32, scores.shape, 0)
    same = own_tile(row, tiles, half) == grouped(scores.shape, 1, patches)
    lifted = jnp.where(same, jnp.exp(scores), 0.0)
    probs = (lifted / jnp.sum(lifted, axis=-1, keepdims=True)).astype(BF16)
    mixed = contract(probs, tokens, 1, 0).astype(BF16)
    for block in range(size):
        blocks[block] = mixed[:, block * rows : (block + 1) * rows]
    for step in range(size):
        outs[step][...] = blocks[other(me, step, size)]


def value_kernel(size, tiles, half, place, *refs):
    parts, (weight, out, mixed) = refs[:size], refs[size:]
    me = place[0] % size
    for step in range(size):
        mixed[source(me, step, size)] = parts[step][...]
    rows = mixed[...].reshape(size * parts[0].shape[0], parts[0].shape[1])
    product = contract(rows, weight[...], 1, 0)
    kept = jnp.where(own_head(product.shape, tiles, half), product, 0.0).astype(BF16)
    spots = (out.shape[0], product.shape[0])
    row = lax.broadcasted_iota(jnp.int32, spots, 1)
    collect = lax.broadcasted_iota(jnp.int32, spots, 0) == own_tile(row, tiles, half)
    out[...] = contract(collect.astype(F32).astype(BF16), kept, 1, 0).astype(BF16)


def embed_kernel(size, place, *refs):
    parts, blocks, (first, project, notes, out, weight) = (
        refs[:size],
        refs[size : 2 * size],
        refs[2 * size :],
    )
    me = place[0] % size
    total = parts[0][...].astype(F32)
    for step in range(1, size):
        total = total + parts[step][...].astype(F32)
    pooled = total.astype(BF16)
    depth = blocks[0].shape[0]
    for step in range(size):
        start = pl.multiple_of(source(me, step, size) * depth, 16)
        weight[pl.ds(start, depth), :] = blocks[step][...]
    class_row = (first[...] + contract(pooled, weight[...], 1, 0)).astype(BF16)
    width = project.shape[1]
    out[:, :width] = contract(class_row, project[...], 1, 0).astype(BF16)
    out[:, width:] = notes[...]


def gather_kernel(*refs):
    parts, out = refs[1:-1], refs[-1]
    total = parts[0][...].astype(F32)
    for part in parts[1:]:
        total = total + part[...].astype(F32)
    width = total.shape[1] - LANES
    there = total[:, width + 2 : width + 3] > 0
    out[:, :width] = jnp.where(there, total[:, :width], 0.0).astype(BF16)
    out[:, width:] = total[:, width:].astype(BF16)


def along_lanes(column):
    shape = (column.shape[0], column.shape[0])
    here = lax.broadcasted_iota(jnp.int32, shape, 0) == lax.broadcasted_iota(jnp.int32, shape, 1)
    return jnp.sum(jnp.where(here, column, 0.0), axis=0, keepdims=True)


def slide_kernel(size, seq_size, place, *refs):
    parts = refs[:seq_size]
    gain, w_query, w_key, w_value = refs[seq_size : seq_size + 4]
    w_out, outs = refs[seq_size + 4 : seq_size + 4 + size], refs[seq_size + 4 + size :]
    me, seq = place[0] % size, place[0] // size
    rows = parts[0].shape[0]
    model = gain.shape[1]
    width = w_query.shape[0]
    total = rows * seq_size
    segment = total // 4
    tiles = jnp.concatenate([part[...].astype(F32) for part in parts], axis=0)
    notes = tiles[:, model:]
    position = along_lanes(notes[:, 0:1] * 256.0 + notes[:, 1:2]).astype(jnp.int32)
    here = along_lanes(notes[:, 2:3])
    normed = normalise(tiles[:, :model], gain[...])
    keys = contract(normed, w_key[...], 1, 1).astype(BF16)
    values = contract(normed, w_value[...], 1, 1).astype(BF16)
    asked = seq * rows + lax.broadcasted_iota(jnp.int32, (rows, total), 0)
    picker = jnp.where(asked == position, 1.0, 0.0).astype(BF16)
    mine = contract(picker, normed, 1, 0).astype(BF16)
    queries = contract(mine, w_query[...], 1, 1).astype(BF16).astype(F32)
    head_size = model // HEADS
    count = width // head_size
    shape = (count, rows, width)
    own = grouped(shape, 2, head_size) == lax.broadcasted_iota(jnp.int32, shape, 0)
    blocked = jnp.where(own, jnp.broadcast_to(queries[None], shape), 0.0)
    blocked = blocked.reshape(count * rows, width).astype(BF16)
    scores = contract(blocked, keys, 1, 1) / math.sqrt(head_size)
    line = lax.broadcasted_iota(jnp.int32, (count * rows, total), 0)
    asking = seq * rows + line % rows
    shift = (me * count + line // rows) % DILATION_STEP
    allowed = (here > 0) | (asking == position)
    near = (asking // segment == position // segment) & allowed
    far = (asking % DILATION_STEP == shift) & (position % DILATION_STEP == shift) & allowed
    times = jnp.where(near, 1.0, 0.0) + jnp.where(far, 1.0, 0.0)
    lifted = jnp.where(times > 0, jnp.exp(scores), 0.0)
    bottom = jnp.sum(lifted * times, axis=-1, keepdims=True)
    weights = (lifted.astype(BF16).astype(F32) * times).astype(BF16)
    mixed = (contract(weights, values, 1, 0) / bottom).reshape(shape)
    attended = jnp.sum(jnp.where(own, mixed, 0.0), axis=0).astype(BF16)
    for step in range(size):
        outs[step][...] = contract(attended, w_out[step][...], 1, 0).astype(BF16)


def residual_kernel(size, seq_size, place, *refs):
    parts, (after, out, blocks) = refs[:seq_size], refs[seq_size:]
    me, seq = place[0] % size, place[0] // size
    rows, width = out.shape
    total = rows * seq_size
    tiles = jnp.concatenate([part[...].astype(F32) for part in parts], axis=0)
    notes = tiles[:, size * width :]
    position = along_lanes(notes[:, 0:1] * 256.0 + notes[:, 1:2]).astype(jnp.int32)
    asked = seq * rows + lax.broadcasted_iota(jnp.int32, (rows, total), 0)
    picker = jnp.where(asked == position, 1.0, 0.0).astype(BF16)
    mine = contract(picker, tiles[:, : size * width].astype(BF16), 1, 0)
    for block in range(size):
        blocks[block] = mine[:, block * width : (block + 1) * width]
    out[...] = blocks[me]


def final_kernel(place, residual, *refs):
    terms, out = refs[:-1], refs[-1]
    total = terms[0][...].astype(F32)
    for term in terms[1:]:
        total = total + term[...].astype(F32)
    out[...] = (residual[...] + total).astype(BF16)


def local(
    tile_patches,
    vit_gain,
    w_query,
    w_key,
    w_value,
    w_out,
    w_proj,
    long_gain,
    long_query,
    long_key,
    long_value,
    long_out,
    seq_order,
    counts,
):
    size = lax.axis_size("fsdp")
    seq_size = lax.axis_size("seq")
    me = lax.axis_index("fsdp")
    place = (lax.axis_index("seq") * size + me).astype(jnp.int32).reshape(1)
    tiles, _, width = tile_patches.shape
    vit_width = w_key.shape[1]
    heads = vit_width // VHD
    rows = w_key.shape[0]
    model = w_proj.shape[1]
    count = tiles * size

    head_row = pl.pallas_call(
        head_kernel,
        out_shape=jax.ShapeDtypeStruct((tiles, width), BF16),
        grid=(1,),
        in_specs=[pl.BlockSpec((tiles, 8, width), lambda i: (0, 0, 0))],
        out_specs=pl.BlockSpec(memory_space=pltpu.VMEM),
        compiler_params=pltpu.CompilerParams(vmem_limit_bytes=1 << 20),
        name="head",
    )(in_hbm(tile_patches))
    head_rows = spread(head_row, "fsdp")
    notes = call(
        functools.partial(notes_kernel, size),
        jax.ShapeDtypeStruct((count, LANES), BF16),
        [pltpu.VMEM((size, tiles, LANES), F32)],
        specs=[pltpu.SMEM, pltpu.SMEM, pl.ANY],
    )(place, seq_order, counts, head_row)

    def cut(weight, after):
        shape = (weight.shape[0], weight.shape[1] // size)
        return call(
            functools.partial(cut_kernel, size),
            [jax.ShapeDtypeStruct(shape, BF16)] * size,
            [pltpu.VMEM((size, *shape), BF16)],
            specs=[pl.ANY],
        )(place, weight, after)

    out_blocks = deal(cut(w_out, head_row), "fsdp")

    normed = normalise(tile_patches.astype(F32), vit_gain)

    gain_row = vit_gain[None, :]

    def halve(weight, after):
        shape = jax.ShapeDtypeStruct((rows, vit_width // 2), BF16)
        kept, sent = call(
            halve_kernel,
            [shape, shape],
            [pltpu.VMEM((2, rows, vit_width // 2), BF16)],
            specs=[pl.ANY],
        )(place, weight, after)
        return kept, swap(sent, "fsdp", 1)

    query_part, first = call(
        functools.partial(query_kernel, size),
        [
            jax.ShapeDtypeStruct((count, vit_width // 2), F32),
            jax.ShapeDtypeStruct((count, rows), F32),
        ],
        [pltpu.VMEM((size, tiles, width), F32), pltpu.VMEM((size, count, rows), F32)],
    )(place, *head_rows, gain_row, *halve(w_query, head_row))
    query_parts = [query_part]
    query_parts += [swap(query_part, "fsdp", step) for step in range(2, size, 2)]

    half = heads // 2
    block = jax.ShapeDtypeStruct((tiles * heads, rows), BF16)
    folded = call(
        functools.partial(fold_kernel, size, half),
        [block] * size,
        [pltpu.VMEM((size, 2, tiles * half, rows), F32)],
    )(place, *query_parts, *halve(w_key, query_part))
    folded = deal(folded, "fsdp")

    mixed = call(
        functools.partial(token_kernel, size, half),
        [block] * size,
        [
            pltpu.VMEM((size, 2, tiles * half, rows), F32),
            pltpu.VMEM((size, tiles * heads, rows), BF16),
            pltpu.VMEM((tiles * heads, width), BF16),
        ],
    )(place, *folded, normed)
    mixed = deal(mixed, "fsdp")

    pooled_part = call(
        functools.partial(value_kernel, size, tiles, half),
        jax.ShapeDtypeStruct((count, vit_width), BF16),
        [pltpu.VMEM((size, tiles * heads, rows), BF16)],
    )(place, *mixed, w_value)
    pooled_parts = spread(pooled_part, "fsdp")

    embed_part = call(
        functools.partial(embed_kernel, size),
        jax.ShapeDtypeStruct((count, model + LANES), BF16),
        [pltpu.VMEM((vit_width, width // size), BF16)],
    )(place, *pooled_parts, *out_blocks, first, w_proj, notes)
    embed_parts = spread(embed_part, "fsdp")

    group_tiles = call(
        gather_kernel, jax.ShapeDtypeStruct((count, model + LANES), BF16)
    )(place, *embed_parts)
    all_tiles = rows_of_all(group_tiles)

    head_width = long_query.shape[1]
    long_blocks = cut(long_out, pooled_part)
    block = jax.ShapeDtypeStruct((count, head_width), BF16)
    terms = call(functools.partial(slide_kernel, size, seq_size), [block] * size)(
        place,
        *all_tiles,
        long_gain[None, :],
        jnp.transpose(long_query),
        jnp.transpose(long_key),
        jnp.transpose(long_value),
        *long_blocks,
    )
    residual = call(
        functools.partial(residual_kernel, size, seq_size),
        jax.ShapeDtypeStruct((count, head_width), F32),
        [pltpu.VMEM((size, count, head_width), F32)],
        specs=[pl.ANY],
    )(place, *all_tiles, terms[0])
    terms = deal(terms, "fsdp")
    return call(
        final_kernel, jax.ShapeDtypeStruct((count, head_width), BF16)
    )(place, residual, *terms)


def solution(mesh):
    return jax.shard_map(
        local,
        mesh=mesh,
        in_specs=(
            P(("group", "seq", "fsdp"), None, None),
            P(),
            P("fsdp", None),
            P("fsdp", None),
            P("fsdp", None),
            P("fsdp", None),
            P("fsdp", None),
            P(),
            P(None, "fsdp"),
            P(None, "fsdp"),
            P(None, "fsdp"),
            P("fsdp", None),
            P(("group", "seq", "fsdp")),
            P(("group", "seq", "fsdp")),
        ),
        out_specs=P(("group", "seq"), "fsdp"),
        check_vma=False,
    )
```

```python
import functools
import math

import jax
import jax.numpy as jnp
from jax import lax
from jax.experimental import pallas as pl
from jax.experimental.pallas import tpu as pltpu
from jax.sharding import PartitionSpec as P


VHD = 64
HEADS = 16
DILATION_STEP = 4
EPSILON = 1e-06
LANES = 128


BF16 = jnp.bfloat16
F32 = jnp.float32


def other(index, step, size):
    return index ^ step if size & (size - 1) == 0 else (index + step) % size


def source(index, step, size):
    return index ^ step if size & (size - 1) == 0 else (index + size - step) % size


def swap(array, axis, step):
    size = lax.axis_size(axis)
    return lax.ppermute(array, axis, [(i, other(i, step, size)) for i in range(size)])


def spread(array, axis):
    return [array] + [swap(array, axis, step) for step in range(1, lax.axis_size(axis))]


def rows_of_all(array):
    size, seq_size = lax.axis_size("fsdp"), lax.axis_size("seq")
    if size % 2 or seq_size & (seq_size - 1) or seq_size < 4:
        return spread(array, "seq")
    pairs = [
        (row * size + place, (row ^ (2 + place % 2)) * size + place)
        for row in range(seq_size)
        for place in range(size)
    ]
    far = lax.ppermute(array, ("seq", "fsdp"), pairs)
    steps = [1, *range(4, seq_size)]
    direct = [swap(array, "seq", step) for step in steps]
    return [array, far, swap(far, "fsdp", 1), *direct]


def deal(arrays, axis):
    return [arrays[0]] + [swap(arrays[step], axis, step) for step in range(1, len(arrays))]


def normalise(rows, gain):
    average = jnp.mean(rows, axis=-1, keepdims=True)
    centred = rows - average
    variance = jnp.mean(centred * centred, axis=-1, keepdims=True)
    return (centred * lax.rsqrt(variance + EPSILON) * gain).astype(BF16)


def contract(left, right, left_axis, right_axis):
    return lax.dot_general(
        left, right, (((left_axis,), (right_axis,)), ((), ())), preferred_element_type=F32
    )


def in_hbm(array):
    return pltpu.with_memory_space_constraint(array, pltpu.HBM)


def call(body, outs, scratch=(), limit=1 << 23, specs=()):
    smem, vmem = pl.BlockSpec(memory_space=pltpu.SMEM), pl.BlockSpec(memory_space=pltpu.VMEM)

    def run(place, *arrays):
        last = len(arrays) - len(specs)
        return pl.pallas_call(
            body,
            out_shape=outs,
            in_specs=[smem] + [vmem] * last + [pl.BlockSpec(memory_space=m) for m in specs],
            out_specs=jax.tree.map(lambda _: vmem, outs),
            scratch_shapes=list(scratch),
            compiler_params=pltpu.CompilerParams(vmem_limit_bytes=limit),
        )(place, *arrays)

    return run


def head_kernel(tokens, out):
    for tile in range(tokens.shape[0]):
        out[tile : tile + 1, :] = tokens[tile, 0:1, :]


def notes_kernel(size, place, order, counts, after, out, rows):
    me = place[0] % size
    tiles = order.shape[0]
    lane = lax.broadcasted_iota(jnp.int32, (1, LANES), 1)
    rows[...] = jnp.zeros_like(rows)
    for tile in range(tiles):
        spot = order[tile]
        present = (counts[0] > tile).astype(jnp.int32)
        high = jnp.where(lane == 0, spot // 256, 0)
        low = jnp.where(lane == 1, spot % 256, 0)
        notes = high + low + jnp.where(lane == 2, present, 0)
        rows[me, tile : tile + 1, :] = notes.astype(F32)
    out[...] = rows[...].reshape(size * tiles, LANES).astype(BF16)


def halve_kernel(place, weight, after, kept, sent, halves):
    mine = place[0] % 2
    half = kept.shape[1]
    for block in range(2):
        halves[block] = weight[:, block * half : (block + 1) * half]
    kept[...] = halves[mine]
    sent[...] = halves[1 - mine]


def query_kernel(size, place, *refs):
    heads_in, (gain, kept, fetched, out, first, rows, blocks) = refs[:size], refs[size:]
    me = place[0] % size
    tiles, width = heads_in[0].shape
    mine = kept.shape[0]
    for step in range(size):
        rows[source(me, step, size)] = heads_in[step][...].astype(F32)
    full = rows[...].reshape(size * tiles, width)
    for block in range(size):
        blocks[block] = full[:, block * mine : (block + 1) * mine]
    first[...] = blocks[me]
    normed = normalise(full, gain[...]).astype(F32)
    for block in range(size):
        blocks[block] = normed[:, block * mine : (block + 1) * mine]
    part = contract(blocks[me].astype(BF16), kept[...], 1, 0)
    part = part + contract(blocks[me ^ 1].astype(BF16), fetched[...], 1, 0)
    out[...] = part


def grouped(shape, axis, span):
    return lax.broadcasted_iota(jnp.int32, shape, axis) // span


def own_head(shape, tiles, half):
    row = lax.broadcasted_iota(jnp.int32, shape, 0)
    return row // (tiles * half) % 2 * half + row % half == grouped(shape, 1, VHD)


def own_tile(row, tiles, half):
    return row // (2 * tiles * half) * tiles + row % (tiles * half) // half


def fold_kernel(size, half, place, *refs):
    parts, (kept, fetched) = refs[: size // 2], refs[size // 2 : size // 2 + 2]
    outs, folded = refs[size // 2 + 2 : -1], refs[-1]
    me = place[0] % size
    total = parts[0][...].astype(F32)
    for part in parts[1:]:
        total = total + part[...].astype(F32)
    count, _ = total.shape
    spots = (count * half, count)
    repeat = grouped(spots, 0, half) == lax.broadcasted_iota(jnp.int32, spots, 1)
    repeated = contract(repeat.astype(F32).astype(BF16), total.astype(BF16), 1, 0)
    shape = repeated.shape
    own = lax.broadcasted_iota(jnp.int32, shape, 0) % half == grouped(shape, 1, VHD)
    blocked = jnp.where(own, repeated, 0.0).astype(BF16)
    for at, weight in ((me % 2, kept), (1 - me % 2, fetched)):
        product = contract(blocked, weight[...], 1, 1)
        product = product.reshape(size, product.shape[0] // size, product.shape[1])
        for owner in range(size):
            folded[owner, at] = product[owner]
    for step in range(size):
        piece = folded[other(me, step, size)]
        outs[step][...] = piece.reshape(outs[step].shape).astype(BF16)


def cut_kernel(size, place, weight, after, *refs):
    outs, blocks = refs[:-1], refs[-1]
    me = place[0] % size
    mine = weight.shape[1] // size
    for block in range(size):
        blocks[block] = weight[:, block * mine : (block + 1) * mine]
    for step in range(size):
        outs[step][...] = blocks[other(me, step, size)]


def token_kernel(size, half, place, *refs):
    parts, normed, outs, (pieces, blocks, folded) = (
        refs[:size],
        refs[size],
        refs[size + 1 : -3],
        refs[-3:],
    )
    me = place[0] % size
    rows = parts[0].shape[1]
    tiles, patches, width = normed.shape
    for step in range(size):
        sender = source(me, step, size)
        at = sender % 2
        part = parts[step][...].astype(F32).reshape(2, tiles * half, rows)
        for block in range(2):
            pieces[sender - at + block, at] = part[block]
    for block in range(size):
        piece = pieces[block].reshape(folded.shape[0], rows).astype(BF16)
        folded[:, block * rows : (block + 1) * rows] = piece
    tokens = normed[...].reshape(tiles * patches, width)
    scores = contract(folded[...], tokens, 1, 1) / math.sqrt(VHD)
    row = lax.broadcasted_iota(jnp.int32, scores.shape, 0)
    same = own_tile(row, tiles, half) == grouped(scores.shape, 1, patches)
    lifted = jnp.where(same, jnp.exp(scores), 0.0)
    probs = (lifted / jnp.sum(lifted, axis=-1, keepdims=True)).astype(BF16)
    mixed = contract(probs, tokens, 1, 0).astype(BF16)
    for block in range(size):
        blocks[block] = mixed[:, block * rows : (block + 1) * rows]
    for step in range(size):
        outs[step][...] = blocks[other(me, step, size)]


def value_kernel(size, tiles, half, place, *refs):
    parts, (weight, out, mixed) = refs[:size], refs[size:]
    me = place[0] % size
    for step in range(size):
        mixed[source(me, step, size)] = parts[step][...]
    rows = mixed[...].reshape(size * parts[0].shape[0], parts[0].shape[1])
    product = contract(rows, weight[...], 1, 0)
    kept = jnp.where(own_head(product.shape, tiles, half), product, 0.0).astype(BF16)
    spots = (out.shape[0], product.shape[0])
    row = lax.broadcasted_iota(jnp.int32, spots, 1)
    collect = lax.broadcasted_iota(jnp.int32, spots, 0) == own_tile(row, tiles, half)
    out[...] = contract(collect.astype(F32).astype(BF16), kept, 1, 0).astype(BF16)


def join_kernel(size, place, *refs):
    blocks, out = refs[:size], refs[-1]
    me = place[0] % size
    depth = blocks[0].shape[0]
    for step in range(size):
        start = pl.multiple_of(source(me, step, size) * depth, 16)
        out[pl.ds(start, depth), :] = blocks[step][...]


def embed_kernel(size, place, *refs):
    parts, (weight, first, project, notes, out) = refs[:size], refs[size:]
    total = parts[0][...].astype(F32)
    for step in range(1, size):
        total = total + parts[step][...].astype(F32)
    pooled = total.astype(BF16)
    class_row = (first[...] + contract(pooled, weight[...], 1, 0)).astype(BF16)
    width = project.shape[1]
    out[:, :width] = contract(class_row, project[...], 1, 0).astype(BF16)
    out[:, width:] = notes[...]


def gather_kernel(*refs):
    parts, out = refs[1:-1], refs[-1]
    total = parts[0][...].astype(F32)
    for part in parts[1:]:
        total = total + part[...].astype(F32)
    width = total.shape[1] - LANES
    there = total[:, width + 2 : width + 3] > 0
    out[:, :width] = jnp.where(there, total[:, :width], 0.0).astype(BF16)
    out[:, width:] = total[:, width:].astype(BF16)


def along_lanes(column):
    shape = (column.shape[0], column.shape[0])
    here = lax.broadcasted_iota(jnp.int32, shape, 0) == lax.broadcasted_iota(jnp.int32, shape, 1)
    return jnp.sum(jnp.where(here, column, 0.0), axis=0, keepdims=True)


def slide_kernel(size, seq_size, place, *refs):
    parts = refs[:seq_size]
    gain, w_query, w_key, w_value = refs[seq_size : seq_size + 4]
    w_out, outs = refs[seq_size + 4 : seq_size + 4 + size], refs[seq_size + 4 + size :]
    me, seq = place[0] % size, place[0] // size
    rows = parts[0].shape[0]
    model = gain.shape[1]
    width = w_query.shape[0]
    total = rows * seq_size
    segment = total // 4
    tiles = jnp.concatenate([part[...].astype(F32) for part in parts], axis=0)
    notes = tiles[:, model:]
    position = along_lanes(notes[:, 0:1] * 256.0 + notes[:, 1:2]).astype(jnp.int32)
    here = along_lanes(notes[:, 2:3])
    normed = normalise(tiles[:, :model], gain[...])
    keys = contract(normed, w_key[...], 1, 1).astype(BF16)
    values = contract(normed, w_value[...], 1, 1).astype(BF16)
    asked = seq * rows + lax.broadcasted_iota(jnp.int32, (rows, total), 0)
    picker = jnp.where(asked == position, 1.0, 0.0).astype(BF16)
    mine = contract(picker, normed, 1, 0).astype(BF16)
    queries = contract(mine, w_query[...], 1, 1).astype(BF16).astype(F32)
    head_size = model // HEADS
    count = width // head_size
    shape = (count, rows, width)
    own = grouped(shape, 2, head_size) == lax.broadcasted_iota(jnp.int32, shape, 0)
    blocked = jnp.where(own, jnp.broadcast_to(queries[None], shape), 0.0)
    blocked = blocked.reshape(count * rows, width).astype(BF16)
    scores = contract(blocked, keys, 1, 1) / math.sqrt(head_size)
    line = lax.broadcasted_iota(jnp.int32, (count * rows, total), 0)
    asking = seq * rows + line % rows
    shift = (me * count + line // rows) % DILATION_STEP
    allowed = (here > 0) | (asking == position)
    near = (asking // segment == position // segment) & allowed
    far = (asking % DILATION_STEP == shift) & (position % DILATION_STEP == shift) & allowed
    times = jnp.where(near, 1.0, 0.0) + jnp.where(far, 1.0, 0.0)
    lifted = jnp.where(times > 0, jnp.exp(scores), 0.0)
    bottom = jnp.sum(lifted * times, axis=-1, keepdims=True)
    weights = (lifted.astype(BF16).astype(F32) * times).astype(BF16)
    mixed = (contract(weights, values, 1, 0) / bottom).reshape(shape)
    attended = jnp.sum(jnp.where(own, mixed, 0.0), axis=0).astype(BF16)
    for step in range(size):
        outs[step][...] = contract(attended, w_out[step][...], 1, 0).astype(BF16)


def residual_kernel(size, seq_size, place, *refs):
    parts, (after, out, blocks) = refs[:seq_size], refs[seq_size:]
    me, seq = place[0] % size, place[0] // size
    rows, width = out.shape
    total = rows * seq_size
    tiles = jnp.concatenate([part[...].astype(F32) for part in parts], axis=0)
    notes = tiles[:, size * width :]
    position = along_lanes(notes[:, 0:1] * 256.0 + notes[:, 1:2]).astype(jnp.int32)
    asked = seq * rows + lax.broadcasted_iota(jnp.int32, (rows, total), 0)
    picker = jnp.where(asked == position, 1.0, 0.0).astype(BF16)
    mine = contract(picker, tiles[:, : size * width].astype(BF16), 1, 0)
    for block in range(size):
        blocks[block] = mine[:, block * width : (block + 1) * width]
    out[...] = blocks[me]


def final_kernel(place, residual, *refs):
    terms, out = refs[:-1], refs[-1]
    total = terms[0][...].astype(F32)
    for term in terms[1:]:
        total = total + term[...].astype(F32)
    out[...] = (residual[...] + total).astype(BF16)


def local(
    tile_patches,
    vit_gain,
    w_query,
    w_key,
    w_value,
    w_out,
    w_proj,
    long_gain,
    long_query,
    long_key,
    long_value,
    long_out,
    seq_order,
    counts,
):
    size = lax.axis_size("fsdp")
    seq_size = lax.axis_size("seq")
    me = lax.axis_index("fsdp")
    place = (lax.axis_index("seq") * size + me).astype(jnp.int32).reshape(1)
    tiles, _, width = tile_patches.shape
    vit_width = w_key.shape[1]
    heads = vit_width // VHD
    rows = w_key.shape[0]
    model = w_proj.shape[1]
    count = tiles * size

    head_row = pl.pallas_call(
        head_kernel,
        out_shape=jax.ShapeDtypeStruct((tiles, width), BF16),
        grid=(1,),
        in_specs=[pl.BlockSpec((tiles, 8, width), lambda i: (0, 0, 0))],
        out_specs=pl.BlockSpec(memory_space=pltpu.VMEM),
        compiler_params=pltpu.CompilerParams(vmem_limit_bytes=1 << 20),
        name="head",
    )(in_hbm(tile_patches))
    head_rows = spread(head_row, "fsdp")
    notes = call(
        functools.partial(notes_kernel, size),
        jax.ShapeDtypeStruct((count, LANES), BF16),
        [pltpu.VMEM((size, tiles, LANES), F32)],
        specs=[pltpu.SMEM, pltpu.SMEM, pl.ANY],
    )(place, seq_order, counts, head_row)

    def cut(weight, after):
        shape = (weight.shape[0], weight.shape[1] // size)
        return call(
            functools.partial(cut_kernel, size),
            [jax.ShapeDtypeStruct(shape, BF16)] * size,
            [pltpu.VMEM((size, *shape), BF16)],
            specs=[pl.ANY],
        )(place, weight, after)

    out_blocks = deal(cut(w_out, head_row), "fsdp")

    normed = normalise(tile_patches.astype(F32), vit_gain)

    gain_row = vit_gain[None, :]

    def halve(weight, after):
        shape = jax.ShapeDtypeStruct((rows, vit_width // 2), BF16)
        kept, sent = call(
            halve_kernel,
            [shape, shape],
            [pltpu.VMEM((2, rows, vit_width // 2), BF16)],
            specs=[pl.ANY],
        )(place, weight, after)
        return kept, swap(sent, "fsdp", 1)

    query_part, first = call(
        functools.partial(query_kernel, size),
        [
            jax.ShapeDtypeStruct((count, vit_width // 2), F32),
            jax.ShapeDtypeStruct((count, rows), F32),
        ],
        [pltpu.VMEM((size, tiles, width), F32), pltpu.VMEM((size, count, rows), F32)],
    )(place, *head_rows, gain_row, *halve(w_query, head_row))
    query_parts = [query_part]
    query_parts += [swap(query_part, "fsdp", step) for step in range(2, size, 2)]

    half = heads // 2
    block = jax.ShapeDtypeStruct((tiles * heads, rows), BF16)
    folded = call(
        functools.partial(fold_kernel, size, half),
        [block] * size,
        [pltpu.VMEM((size, 2, tiles * half, rows), F32)],
    )(place, *query_parts, *halve(w_key, query_part))
    folded = deal(folded, "fsdp")

    mixed = call(
        functools.partial(token_kernel, size, half),
        [block] * size,
        [
            pltpu.VMEM((size, 2, tiles * half, rows), F32),
            pltpu.VMEM((size, tiles * heads, rows), BF16),
            pltpu.VMEM((tiles * heads, width), BF16),
        ],
    )(place, *folded, normed)
    mixed = deal(mixed, "fsdp")

    pooled_part = call(
        functools.partial(value_kernel, size, tiles, half),
        jax.ShapeDtypeStruct((count, vit_width), BF16),
        [pltpu.VMEM((size, tiles * heads, rows), BF16)],
    )(place, *mixed, w_value)
    pooled_parts = spread(pooled_part, "fsdp")

    out_weight = call(
        functools.partial(join_kernel, size),
        jax.ShapeDtypeStruct((vit_width, width // size), BF16),
        specs=[pl.ANY],
    )(place, *out_blocks, pooled_part)
    embed_part = call(
        functools.partial(embed_kernel, size), jax.ShapeDtypeStruct((count, model + LANES), BF16)
    )(place, *pooled_parts, out_weight, first, w_proj, notes)
    embed_parts = spread(embed_part, "fsdp")

    group_tiles = call(
        gather_kernel, jax.ShapeDtypeStruct((count, model + LANES), BF16)
    )(place, *embed_parts)
    all_tiles = rows_of_all(group_tiles)

    head_width = long_query.shape[1]
    long_blocks = cut(long_out, pooled_part)
    block = jax.ShapeDtypeStruct((count, head_width), BF16)
    terms = call(functools.partial(slide_kernel, size, seq_size), [block] * size)(
        place,
        *all_tiles,
        long_gain[None, :],
        jnp.transpose(long_query),
        jnp.transpose(long_key),
        jnp.transpose(long_value),
        *long_blocks,
    )
    residual = call(
        functools.partial(residual_kernel, size, seq_size),
        jax.ShapeDtypeStruct((count, head_width), F32),
        [pltpu.VMEM((size, count, head_width), F32)],
        specs=[pl.ANY],
    )(place, *all_tiles, terms[0])
    terms = deal(terms, "fsdp")
    return call(
        final_kernel, jax.ShapeDtypeStruct((count, head_width), BF16)
    )(place, residual, *terms)


def solution(mesh):
    return jax.shard_map(
        local,
        mesh=mesh,
        in_specs=(
            P(("group", "seq", "fsdp"), None, None),
            P(),
            P("fsdp", None),
            P("fsdp", None),
            P("fsdp", None),
            P("fsdp", None),
            P("fsdp", None),
            P(),
            P(None, "fsdp"),
            P(None, "fsdp"),
            P(None, "fsdp"),
            P("fsdp", None),
            P(("group", "seq", "fsdp")),
            P(("group", "seq", "fsdp")),
        ),
        out_specs=P(("group", "seq"), "fsdp"),
        check_vma=False,
    )
```
